512 devices in a mesh: ctx: 32 (over y, x, core), ch: 16 (over z).
Axes of the slice: x: 4, y: 4, z: 16, core: 2. Of those that a mesh axis runs over, the one named last changes fastest.
Arguments:
- stream: bfloat16 [16384, 4096], P('ctx', 'ch'), may hold values from -900 to 900
- key_gate: bfloat16 [16384, 4096], P('ctx', 'ch'), may hold values from -6 to 6
- query_gate: bfloat16 [16384, 4096], P('ctx', 'ch'), may hold values from -6 to 6
- grad_output: bfloat16 [16384, 4096], P('ctx', 'ch'), may hold values from -50 to 50
- norm_gain: float32 [4096], P('ch'), may hold values from 0.1 to 1.9
- residue: float32 [4096, 16], P('ch'), may hold values from -0.5 to 0.5
- log_rate: float32 [4096, 16], P('ch'), may hold values from -14 to -2.9
Outputs:
- output: bfloat16 [16384, 4096], P('ctx', 'ch')
- grad_stream: bfloat16 [16384, 4096], P('ctx', 'ch')
- grad_key: bfloat16 [16384, 4096], P('ctx', 'ch')
- grad_query: bfloat16 [16384, 4096], P('ctx', 'ch')
- grad_gain: float32 [4096], P('ch')
- grad_residue: float32 [4096, 16], P('ch')
- grad_rate: float32 [4096, 16], P('ch')
The draws below stay inside these ranges and needn't reach their ends.
All inputs are finite; a program needn't handle non-finite values.
Results may differ from the reference program's by a relative error of at most 0.008.
Values sent between devices are 32-bit elements; how exact they have to be, the bound alone decides.
No kernel may reach another device: no remote copies, remote signals or barrier semaphores. Data moves between devices by JAX's collectives and lax.ppermute only.
A program may use at most 128 MiB of HBM per device.

```python
import math
import jax
import jax.numpy as jnp
from jax import lax

D = 4096
MODES = 16
SEQ = 16384


def draw_stream(key, part):
    keys = jax.random.split(key, 3)
    base = jnp.clip(jax.random.normal(keys[0], (SEQ, D), jnp.float32), -6.0, 6.0)
    row_log = jax.random.uniform(keys[1], (SEQ, 1), jnp.float32, 0.0, math.log(10.0))
    col_log = math.log(10.0) * jnp.arange(D, dtype=jnp.float32)[None, :] / D
    col_log = col_log + jax.random.uniform(keys[2], (1, D), jnp.float32, -0.25, 0.25)
    return (base * jnp.exp(row_log) * jnp.exp(col_log)).astype(jnp.bfloat16)


def draw_grad_output(key, part):
    keys = jax.random.split(key, 2)
    position = jnp.arange(SEQ, dtype=jnp.float32)[:, None] / SEQ
    base = jnp.clip(jax.random.normal(keys[0], (SEQ, D), jnp.float32), -6.0, 6.0)
    rising = math.log(3.0) * position
    jitter = jax.random.uniform(keys[1], (SEQ, 1), jnp.float32, -0.3, 0.3)
    return (base * jnp.exp(rising + jitter)).astype(jnp.bfloat16)


def mode_draw(key):
    keys = jax.random.split(jax.random.fold_in(key, 11), 5)
    shape = (D, MODES)
    picker = jax.random.uniform(keys[0], shape, jnp.float32)
    slow = jnp.exp(jax.random.uniform(keys[1], shape, jnp.float32, math.log(0.1 / SEQ), math.log(2.0 / SEQ)))
    middle = jnp.exp(jax.random.uniform(keys[2], shape, jnp.float32, math.log(2.0 / SEQ), math.log(1.0 / 50.0)))
    fast = jnp.exp(jax.random.uniform(keys[3], shape, jnp.float32, math.log(1.0 / 50.0), math.log(1.0 / 20.0)))
    decay_rate = jnp.where(picker < 0.5, slow, jnp.where(picker < 0.75, middle, fast))
    factor = jnp.clip(jax.random.normal(keys[4], shape, jnp.float32), -6.0, 6.0)
    residue = factor * jnp.sqrt((2.0 * decay_rate + 2.0 / SEQ) / MODES)
    return (jnp.log(decay_rate), residue)


def draw_residue(key, part):
    return mode_draw(key)[1].astype(jnp.float32)


def draw_log_rate(key, part):
    return mode_draw(key)[0].astype(jnp.float32)


def block_scale(key, dims, cuts, least, high):
    level, own = 1.0, jax.random.fold_in(key, 6)
    for axis_at, blocks in cuts:
        steps = jnp.exp(jax.random.uniform(jax.random.fold_in(own, axis_at), (blocks,), jnp.float32, least / len(cuts), high / len(cuts)))
        level = level * jnp.repeat(steps, dims[axis_at] // blocks).reshape([-1 if axis == axis_at else 1 for axis in range(len(dims))])
    return level


def scatter_about(own_key, shape, deviation, reach, cuts=(), kind=jnp.bfloat16):
    loudness = block_scale(own_key, shape, cuts, -0.22, 0.18) if cuts else 1.0
    entries = jax.random.normal(own_key, shape, jnp.float32) * deviation * loudness
    return jnp.minimum(jnp.maximum(entries, -reach), reach).astype(kind)


def setup_inputs(seed: int = 0) -> dict:
    key_of = jax.random.split(jax.random.key(seed), 8)
    stream = draw_stream(jax.random.fold_in(key_of[7], 71), 0)
    key_gate = scatter_about(key_of[1], (SEQ, D), 1.0, 6.0, ((0, 32), (1, 16)))
    query_gate = scatter_about(key_of[2], (SEQ, D), 1.0, 6.0, ((0, 32), (1, 16)))
    grad_output = draw_grad_output(jax.random.fold_in(key_of[7], 71), 0)
    norm_gain = jnp.clip(1.0 + 0.18 * jax.random.normal(key_of[4], (D,), jnp.float32), 0.1, 1.9)
    residue = draw_residue(jax.random.fold_in(key_of[7], 71), 0)
    log_rate = draw_log_rate(jax.random.fold_in(key_of[7], 71), 0)
    return {"stream": stream, "key_gate": key_gate, "query_gate": query_gate, "grad_output": grad_output, "norm_gain": norm_gain, "residue": residue, "log_rate": log_rate}


epsilon = 1e-05

def filter_group(signal, grad_conv, residue, log_rate):
    length = signal.shape[1]
    decay_rate = jnp.exp(log_rate)
    lags = jnp.arange(length, dtype=jnp.float32)
    powers = jnp.exp(-decay_rate[:, :, None] * lags)
    kernel = jnp.einsum('cm,cmd->cd', residue, powers, precision=lax.Precision.HIGHEST)
    fft_size = 2 * length
    spec_signal = jnp.fft.rfft(signal, fft_size, axis=1)
    spec_kernel = jnp.fft.rfft(kernel, fft_size, axis=1)
    spec_grad = jnp.fft.rfft(grad_conv, fft_size, axis=1)
    conv = jnp.fft.irfft(spec_signal * spec_kernel, fft_size, axis=1)[:, :length]
    grad_signal = jnp.fft.irfft(jnp.conj(spec_kernel) * spec_grad, fft_size, axis=1)[:, :length]
    grad_kernel = jnp.fft.irfft(jnp.conj(spec_signal) * spec_grad, fft_size, axis=1)[:, :length]
    grad_residue = jnp.einsum('cd,cmd->cm', grad_kernel, powers, precision=lax.Precision.HIGHEST)
    weighted = jnp.einsum('cd,cmd->cm', grad_kernel * lags, powers, precision=lax.Precision.HIGHEST)
    grad_rate = -decay_rate * residue * weighted
    return (conv, grad_signal, grad_residue, grad_rate)

def reference(stream, key_gate, query_gate, grad_output, norm_gain, residue, log_rate):
    wide_stream = stream.astype(jnp.float32)
    inv_rms = lax.rsqrt(lax.optimization_barrier(jnp.mean(wide_stream * wide_stream, axis=1, keepdims=True)) + epsilon)
    unit_stream = wide_stream * inv_rms
    normed = unit_stream * norm_gain
    key_wide = key_gate.astype(jnp.float32)
    query_wide = query_gate.astype(jnp.float32)
    grad_wide = grad_output.astype(jnp.float32)
    signal = (key_wide * normed).astype(jnp.bfloat16)
    grad_conv = grad_wide * query_wide
    length, channels = stream.shape
    group_size = min(64, channels)
    groups = channels // group_size

    def per_group(items):
        return filter_group(items[0], items[1], items[2], items[3])
    results = lax.map(per_group, (signal.astype(jnp.float32).T.reshape(groups, group_size, length), grad_conv.T.reshape(groups, group_size, length), residue.reshape(groups, group_size, MODES), log_rate.reshape(groups, group_size, MODES)))
    conv = results[0].reshape(channels, length).T
    grad_signal = results[1].reshape(channels, length).T
    scale = 1.0 / math.sqrt(SEQ)
    grad_residue = results[2].reshape(channels, MODES) * scale
    grad_rate = results[3].reshape(channels, MODES) * scale
    output = (query_wide * conv).astype(jnp.bfloat16)
    grad_query = (grad_wide * conv).astype(jnp.bfloat16)
    grad_key = (grad_signal * normed).astype(jnp.bfloat16)
    grad_normed = grad_signal * key_wide
    grad_gain = lax.optimization_barrier(jnp.sum(grad_normed * unit_stream, axis=0)) * scale
    grad_unit = grad_normed * norm_gain
    inner = lax.optimization_barrier(jnp.sum(grad_unit * unit_stream, axis=1, keepdims=True)) / D
    grad_stream = (inv_rms * (grad_unit - unit_stream * inner)).astype(jnp.bfloat16)
    return (output, grad_stream, grad_key, grad_query, grad_gain, grad_residue, grad_rate)
```

```python
import math

import jax
import jax.numpy as jnp
from jax import lax
from jax.experimental import pallas as pl
from jax.experimental.pallas import tpu as pltpu
from jax.sharding import PartitionSpec as P

D = 4096
MODES = 16
ROWS = 512
COLS = 256
CHUNKS = 32
CH = 16
LANES = 128
SUB = 8
BLOCKS = ROWS // SUB
HALVES = COLS // LANES
GROUPS = MODES // SUB
epsilon = 1e-05
highest = lax.Precision.HIGHEST
f32 = jnp.float32
bf16 = jnp.bfloat16


def call(kernel, outs, scratch=(), flops=1 << 22, name=None):
    return pl.pallas_call(
        kernel,
        out_shape=tuple(jax.ShapeDtypeStruct(s, d) for s, d in outs),
        scratch_shapes=list(scratch),
        cost_estimate=pl.CostEstimate(flops=flops, bytes_accessed=1 << 21, transcendentals=0),
        name=name,
    )


def lane(half):
    return pl.ds(half * LANES, LANES)


def lane_slice(half):
    return slice(half * LANES, (half + 1) * LANES)


def tiles(ref):
    return [[ref[g * SUB : (g + 1) * SUB, lane(h)] for h in range(HALVES)] for g in range(GROUPS)]


def each(fn, *args):
    return [[fn(*(a[g][h] for a in args)) for h in range(HALVES)] for g in range(GROUPS)]


def zeros_tiles():
    return [[jnp.zeros((SUB, LANES), f32) for _ in range(HALVES)] for _ in range(GROUPS)]


def fold_sublanes(parts):
    sub = lax.broadcasted_iota(jnp.int32, (SUB, LANES), 0)
    low4 = sub < 4
    low2 = (sub & 2) == 0
    low1 = (sub & 1) == 0
    four = []
    for k in range(4):
        a, b = parts[k], parts[k + 4]
        four.append(jnp.where(low4, a, b) + pltpu.roll(jnp.where(low4, b, a), 4, 0))
    two = []
    for k in range(2):
        a, b = four[k], four[k + 2]
        two.append(jnp.where(low2, a + pltpu.roll(a, 6, 0), b + pltpu.roll(b, 2, 0)))
    a, b = two
    return jnp.where(low1, a + pltpu.roll(a, 7, 0), b + pltpu.roll(b, 1, 0))


def row(ref, t, half):
    return ref[pl.ds(half * ROWS + t, SUB, stride=0), :]


def span(start, size, half):
    return (pl.ds(half * ROWS + start, size), slice(None))


def send_rows(ref, total):
    sub = lax.broadcasted_iota(jnp.int32, (SUB, LANES), 0) & 3
    parts = [total[:, k * LANES : (k + 1) * LANES] for k in range(4)]
    tile = jnp.where(
        sub == 0, parts[0], jnp.where(sub == 1, parts[1], jnp.where(sub == 2, parts[2], parts[3]))
    )
    ref[...] = jnp.broadcast_to(tile[None], (CH, SUB, LANES))


def lane_sums(values):
    ones = jnp.ones((SUB, LANES), f32)
    return lax.dot_general(
        ones, values, (((1,), (1,)), ((), ())), precision=highest, preferred_element_type=f32
    )


def columns(tile):
    turned = tile.T
    return [turned[:, k : k + 1] for k in range(4)]


def square_kernel(stream_ref, send_ref):
    wide = [stream_ref[:, lane(h)].astype(f32) for h in range(HALVES)]
    send_rows(send_ref, lane_sums(sum(v * v for v in wide)))


def adjoint_kernel(
    query_ref, grad_ref, log_rate_ref, residue_ref, g_ref, local_ref, p_ref, w_ref
):
    for h in range(HALVES):
        g_ref[span(0, ROWS, h)] = grad_ref[:, lane(h)].astype(f32) * query_ref[
            :, lane(h)
        ].astype(f32)
    lam = each(lambda v: jnp.exp(-jnp.exp(v)), tiles(log_rate_ref))
    res = tiles(residue_ref)

    def block(i, carry):
        p, w = carry
        base = pl.multiple_of((BLOCKS - 1 - i) * SUB, SUB)
        parts = [[None] * SUB for _ in range(HALVES)]
        for k in reversed(range(SUB)):
            rows = [row(g_ref, base + k, h) for h in range(HALVES)]
            a = each(lambda l, v: l * v, lam, p)
            w = each(lambda l, v, c: l * v + c, lam, w, a)
            p = [[a[g][h] + rows[h] for h in range(HALVES)] for g in range(GROUPS)]
            for h in range(HALVES):
                parts[h][k] = res[0][h] * p[0][h] + res[1][h] * p[1][h]
        for h in range(HALVES):
            local_ref[span(base, SUB, h)] = fold_sublanes(parts[h])
        return p, w

    p, w = lax.fori_loop(0, BLOCKS, block, (zeros_tiles(), zeros_tiles()))
    for g in range(GROUPS):
        for h in range(HALVES):
            p_ref[g * SUB : (g + 1) * SUB, lane(h)] = p[g][h]
            w_ref[g * SUB : (g + 1) * SUB, lane(h)] = w[g][h]


def state_kernel(
    recv_ref,
    stream_ref,
    key_ref,
    gain_ref,
    g_ref,
    local_ref,
    p_ref,
    w_ref,
    log_rate_ref,
    send_ref,
    x_ref,
    unit_ref,
    inv_ref,
    u_ref,
):
    total = jnp.sum(recv_ref[...], axis=0)
    inverse = columns(lax.rsqrt(total / D + epsilon))
    gain = gain_ref[...]
    for k in range(4):
        part = pl.ds(k * LANES, LANES)
        inv = jnp.broadcast_to(inverse[k], (LANES, LANES))
        inv_ref[part, :] = inv
        for h in range(HALVES):
            unit = stream_ref[part, lane(h)].astype(f32) * inv
            key = key_ref[part, lane(h)].astype(f32)
            own = span(k * LANES, LANES, h)
            unit_ref[own] = unit
            u_ref[own] = key * unit
            signal = key * (unit * gain[:, lane_slice(h)])
            x_ref[own] = signal.astype(bf16).astype(f32)
    lam = each(lambda v: jnp.exp(-jnp.exp(v)), tiles(log_rate_ref))

    def block(i, carry):
        state, moment, plain, first, second, gains = carry
        base = pl.multiple_of(i * SUB, SUB)
        for k in range(SUB):
            xs = [row(x_ref, base + k, h) for h in range(HALVES)]
            us = [row(u_ref, base + k, h) for h in range(HALVES)]
            gs = [row(g_ref, base + k, h) for h in range(HALVES)]
            a = each(lambda l, v: l * v, lam, state)
            moment = each(lambda l, v, c: l * v + c, lam, moment, a)
            state = [[a[g][h] + xs[h] for h in range(HALVES)] for g in range(GROUPS)]
            plain = [
                [lam[g][h] * plain[g][h] + us[h] for h in range(HALVES)] for g in range(GROUPS)
            ]
            first = [
                [first[g][h] + gs[h] * state[g][h] for h in range(HALVES)] for g in range(GROUPS)
            ]
            second = [
                [second[g][h] + gs[h] * moment[g][h] for h in range(HALVES)]
                for g in range(GROUPS)
            ]
        gains = [
            gains[h] + u_ref[span(base, SUB, h)] * local_ref[span(base, SUB, h)]
            for h in range(HALVES)
        ]
        return state, moment, plain, first, second, gains

    zero = zeros_tiles
    start = (zero(), zero(), zero(), zero(), zero(), zero()[0])
    state, moment, plain, first, second, gains = lax.fori_loop(0, BLOCKS, block, start)
    last = [gains, [jnp.zeros((SUB, LANES), f32)] * HALVES]
    sent = [state, plain, moment, tiles(p_ref), tiles(w_ref), first, second, last]
    for q in range(SUB):
        for g in range(GROUPS):
            for h in range(HALVES):
                at = g * SUB * HALVES * SUB + h * SUB + q
                send_ref[pl.ds(at, SUB, stride=HALVES * SUB), :] = sent[q][g][h]


def shifted(value, k):
    index = lax.broadcasted_iota(jnp.int32, (CHUNKS, LANES), 0)
    return jnp.where(index >= k, pltpu.roll(value, k, 0), 0.0)


def shifted_back(value, k):
    index = lax.broadcasted_iota(jnp.int32, (CHUNKS, LANES), 0)
    return jnp.where(index < CHUNKS - k, pltpu.roll(value, CHUNKS - k, 0), 0.0)


def owner_kernel(recv_ref, log_rate_ref, residue_ref, send_ref):
    state, plain, moment, p, w, first, second, gains = (
        recv_ref[pl.ds(q, CHUNKS, stride=SUB), :] for q in range(SUB)
    )
    rate = jnp.exp(log_rate_ref[...])
    res = residue_ref[...]
    lam = jnp.exp(-rate)
    whole, whole_u, whole_q, back = state, plain, moment, p
    for step in (1, 2, 4, 8, 16):
        far = jnp.exp(rate * (-float(ROWS * step)))
        before = shifted(whole, step)
        whole_q = whole_q + far * (shifted(whole_q, step) + float(ROWS * step) * before)
        whole = whole + far * before
        whole_u = whole_u + far * shifted(whole_u, step)
        back = back + far * shifted_back(back, step)
    into, into_u, into_q = shifted(whole, 1), shifted(whole_u, 1), shifted(whole_q, 1)
    into_p = shifted_back(back, 1)
    scale = 1.0 / math.sqrt(ROWS * CHUNKS)
    grad_residue = jnp.sum(first + lam * (into * p), axis=0, keepdims=True)
    weighted = jnp.sum(second + lam * ((w + p) * into + p * into_q), axis=0, keepdims=True)
    grad_gain = jnp.sum(gains + res * (lam * (into_u * p)), axis=0, keepdims=True)
    shape = (CHUNKS, LANES)
    rows = [
        into,
        into_p,
        jnp.broadcast_to(grad_residue * scale, shape),
        jnp.broadcast_to(-rate * res * weighted * scale, shape),
        jnp.broadcast_to(grad_gain * scale, shape),
    ]
    rows += [jnp.zeros(shape, f32)] * (SUB - len(rows))
    for q in range(SUB):
        send_ref[pl.ds(q, CHUNKS, stride=SUB), :] = rows[q]


def received(ref, q):
    stride = HALVES * SUB
    return [
        [
            ref[pl.ds(g * SUB * stride + h * SUB + q, SUB, stride=stride), :]
            for h in range(HALVES)
        ]
        for g in range(GROUPS)
    ]


def correct_kernel(
    recv_ref,
    local_ref,
    unit_ref,
    key_ref,
    gain_ref,
    log_rate_ref,
    residue_ref,
    send_ref,
    total_ref,
):
    lam = each(lambda v: jnp.exp(-jnp.exp(v)), tiles(log_rate_ref))
    start = each(lambda r, v: r * v, tiles(residue_ref), received(recv_ref, 1))

    def block(i, state):
        base = pl.multiple_of((BLOCKS - 1 - i) * SUB, SUB)
        parts = [[None] * SUB for _ in range(HALVES)]
        for k in reversed(range(SUB)):
            state = each(lambda l, v: l * v, lam, state)
            for h in range(HALVES):
                parts[h][k] = state[0][h] + state[1][h]
        for h in range(HALVES):
            at = span(base, SUB, h)
            total_ref[at] = local_ref[at] + fold_sublanes(parts[h])
        return state

    lax.fori_loop(0, BLOCKS, block, start)
    gain = gain_ref[...]
    products = []
    for h in range(HALVES):
        at = span(0, ROWS, h)
        grad_unit = total_ref[at] * key_ref[:, lane(h)].astype(f32) * gain[:, lane_slice(h)]
        products.append(grad_unit * unit_ref[at])
    send_rows(send_ref, lane_sums(sum(products)))


def forward_kernel(
    recv_ref,
    x_ref,
    unit_ref,
    inv_ref,
    total_ref,
    key_ref,
    query_ref,
    grad_ref,
    gain_ref,
    log_rate_ref,
    residue_ref,
    output_ref,
    grad_key_ref,
    grad_query_ref,
    left_ref,
    right_ref,
    grad_residue_ref,
    grad_rate_ref,
    grad_gain_ref,
    conv_ref,
):
    lam = each(lambda v: jnp.exp(-jnp.exp(v)), tiles(log_rate_ref))
    res = tiles(residue_ref)

    def block(i, state):
        base = pl.multiple_of(i * SUB, SUB)
        parts = [[None] * SUB for _ in range(HALVES)]
        for k in range(SUB):
            xs = [row(x_ref, base + k, h) for h in range(HALVES)]
            state = [
                [lam[g][h] * state[g][h] + xs[h] for h in range(HALVES)] for g in range(GROUPS)
            ]
            for h in range(HALVES):
                parts[h][k] = res[0][h] * state[0][h] + res[1][h] * state[1][h]
        for h in range(HALVES):
            conv_ref[span(base, SUB, h)] = fold_sublanes(parts[h])
        return state

    lax.fori_loop(0, BLOCKS, block, received(recv_ref, 0))
    gain = gain_ref[...]
    for k in range(4):
        part = pl.ds(k * LANES, LANES)
        inv = inv_ref[part, :]
        for h in range(HALVES):
            at = (part, lane(h))
            own = span(k * LANES, LANES, h)
            conv = conv_ref[own]
            output_ref[at] = (query_ref[at].astype(f32) * conv).astype(bf16)
            grad_query_ref[at] = (grad_ref[at].astype(f32) * conv).astype(bf16)
            unit = unit_ref[own]
            total = total_ref[own]
            own_gain = gain[:, lane_slice(h)]
            grad_key_ref[at] = (total * (unit * own_gain)).astype(bf16)
            left_ref[own] = inv * (total * key_ref[at].astype(f32) * own_gain)
            right_ref[own] = inv * unit
    for q, ref in ((2, grad_residue_ref), (3, grad_rate_ref)):
        found = received(recv_ref, q)
        for g in range(GROUPS):
            for h in range(HALVES):
                ref[g * SUB : (g + 1) * SUB, lane(h)] = found[g][h]
    found = received(recv_ref, 4)
    for h in range(HALVES):
        grad_gain_ref[:, lane(h)] = jnp.sum(found[0][h] + found[1][h], axis=0, keepdims=True)


def finish_kernel(recv_ref, left_ref, right_ref, grad_stream_ref):
    inner = columns(jnp.sum(recv_ref[...], axis=0) / D)
    for k in range(4):
        part = pl.ds(k * LANES, LANES)
        across = jnp.broadcast_to(inner[k], (LANES, LANES))
        for h in range(HALVES):
            own = span(k * LANES, LANES, h)
            value = left_ref[own] - right_ref[own] * across
            grad_stream_ref[part, lane(h)] = value.astype(bf16)


def exchange(value, axis):
    return lax.all_to_all(value, axis, split_axis=0, concat_axis=0, tiled=True)


def local(stream, key_gate, query_gate, grad_output, norm_gain, residue, log_rate):
    wide = (ROWS, COLS)
    split = (HALVES * ROWS, LANES)
    modes = (MODES, COLS)
    tile = (CH, SUB, LANES)
    packed = (CHUNKS * SUB, LANES)
    (squares,) = call(square_kernel, [(tile, f32)], name="square")(stream)
    squares = exchange(squares, "ch")
    log_rate_t = log_rate.T
    residue_t = residue.T
    gain = norm_gain[None, :]
    me = lax.axis_index("ctx")
    log_rate_own = lax.dynamic_slice_in_dim(log_rate_t.reshape(CHUNKS, LANES), me, 1, 0)
    residue_own = lax.dynamic_slice_in_dim(residue_t.reshape(CHUNKS, LANES), me, 1, 0)
    grad_conv, local_grad, p, w = call(
        adjoint_kernel, [(split, f32), (split, f32), (modes, f32), (modes, f32)], name="adjoint"
    )(query_gate, grad_output, log_rate_t, residue_t)
    sent, signal, unit, inv = call(
        state_kernel,
        [(packed, f32), (split, f32), (split, f32), ((ROWS, LANES), f32)],
        [pltpu.VMEM(split, f32)],
        name="state",
    )(squares, stream, key_gate, gain, grad_conv, local_grad, p, w, log_rate_t)
    got = exchange(sent.reshape(CHUNKS, SUB, LANES), "ctx").reshape(packed)
    (sent,) = call(owner_kernel, [(packed, f32)], name="owner")(got, log_rate_own, residue_own)
    got = exchange(sent.reshape(CHUNKS, SUB, LANES), "ctx").reshape(packed)
    inner, total = call(
        correct_kernel, [(tile, f32), (split, f32)], name="correct"
    )(got, local_grad, unit, key_gate, gain, log_rate_t, residue_t)
    inner = exchange(inner, "ch")
    output, grad_key, grad_query, left, right, grad_residue, grad_rate, grad_gain = call(
        forward_kernel,
        [
            (wide, bf16),
            (wide, bf16),
            (wide, bf16),
            (split, f32),
            (split, f32),
            (modes, f32),
            (modes, f32),
            ((1, COLS), f32),
        ],
        [pltpu.VMEM(split, f32)],
        name="forward",
    )(
        got,
        signal,
        unit,
        inv,
        total,
        key_gate,
        query_gate,
        grad_output,
        gain,
        log_rate_t,
        residue_t,
    )
    (grad_stream,) = call(finish_kernel, [(wide, bf16)], name="finish")(inner, left, right)
    return (
        output,
        grad_stream,
        grad_key,
        grad_query,
        grad_gain[0],
        grad_residue.T,
        grad_rate.T,
    )


def solution(mesh):
    placed = (
        P("ctx", "ch"),
        P("ctx", "ch"),
        P("ctx", "ch"),
        P("ctx", "ch"),
        P("ch"),
        P("ch", None),
        P("ch", None),
    )
    return jax.shard_map(
        local,
        mesh=mesh,
        in_specs=placed,
        out_specs=(
            P("ctx", "ch"),
            P("ctx", "ch"),
            P("ctx", "ch"),
            P("ctx", "ch"),
            P("ch"),
            P("ch", None),
            P("ch", None),
        ),
        check_vma=False,
    )
```

```python
import math

import jax
import jax.numpy as jnp
from jax import lax
from jax.experimental import pallas as pl
from jax.experimental.pallas import tpu as pltpu
from jax.sharding import PartitionSpec as P

D = 4096
MODES = 16
ROWS = 512
COLS = 256
CHUNKS = 32
CH = 16
LANES = 128
SUB = 8
BLOCKS = ROWS // SUB
SPAN = 64
HALVES = COLS // LANES
GROUPS = MODES // SUB
epsilon = 1e-05
f32 = jnp.float32
bf16 = jnp.bfloat16


def call(kernel, count, outs, scratch=(), flops=1 << 22, name=None):
    held = pl.BlockSpec(memory_space=pltpu.VMEM)
    return pl.pallas_call(
        kernel,
        in_specs=[held] * count,
        out_specs=tuple([held] * len(outs)),
        out_shape=tuple(jax.ShapeDtypeStruct(s, d) for s, d in outs),
        scratch_shapes=list(scratch),
        cost_estimate=pl.CostEstimate(flops=flops, bytes_accessed=1 << 21, transcendentals=0),
        name=name,
    )


def lane(half):
    return pl.ds(half * LANES, LANES)


def lane_slice(half):
    return slice(half * LANES, (half + 1) * LANES)


def tiles(ref):
    return [[ref[g * SUB : (g + 1) * SUB, lane(h)] for h in range(HALVES)] for g in range(GROUPS)]


def each(fn, *args):
    return [[fn(*(a[g][h] for a in args)) for h in range(HALVES)] for g in range(GROUPS)]


def zeros_tiles():
    return [[jnp.zeros((SUB, LANES), f32) for _ in range(HALVES)] for _ in range(GROUPS)]


def fold_sublanes(parts):
    sub = lax.broadcasted_iota(jnp.int32, (SUB, LANES), 0)
    low4 = sub < 4
    low2 = (sub & 2) == 0
    low1 = (sub & 1) == 0
    four = []
    for k in range(4):
        a, b = parts[k], parts[k + 4]
        four.append(jnp.where(low4, a, b) + pltpu.roll(jnp.where(low4, b, a), 4, 0))
    two = []
    for k in range(2):
        a, b = four[k], four[k + 2]
        two.append(jnp.where(low2, a + pltpu.roll(a, 6, 0), b + pltpu.roll(b, 2, 0)))
    a, b = two
    return jnp.where(low1, a + pltpu.roll(a, 7, 0), b + pltpu.roll(b, 1, 0))


def row(ref, t, half):
    return ref[pl.ds(half * ROWS + t, SUB, stride=0), :]


def span(start, size, half):
    return (pl.ds(half * ROWS + start, size), slice(None))


def send_rows(ref, values):
    sub = lax.broadcasted_iota(jnp.int32, (SUB, LANES), 0) & 3
    tile = None
    for k in range(4):
        turned = values[k * LANES : (k + 1) * LANES].T
        part = jnp.broadcast_to(jnp.sum(turned, axis=0, keepdims=True), (SUB, LANES))
        tile = part if tile is None else jnp.where(sub == k, part, tile)
    ref[...] = jnp.broadcast_to(tile[None], (CH, SUB, LANES))


def columns(tile):
    turned = tile.T
    return [turned[:, k : k + 1] for k in range(4)]


def square_kernel(stream_ref, send_ref):
    wide = [stream_ref[:, lane(h)].astype(f32) for h in range(HALVES)]
    send_rows(send_ref, sum(v * v for v in wide))


def tile_rows(start, group, half):
    return pl.ds(start + (group * HALVES + half) * SUB, SUB)


def adjoint_kernel(
    query_ref,
    grad_ref,
    log_rate_ref,
    residue_ref,
    g_ref,
    local_ref,
    p_ref,
    w_ref,
    across_ref,
    across_lag_ref,
    lagged_ref,
    fade_ref,
    rate_ref,
    weight_ref,
):
    for h in range(HALVES):
        g_ref[span(0, ROWS, h)] = grad_ref[:, lane(h)].astype(f32) * query_ref[
            :, lane(h)
        ].astype(f32)
    rate = each(jnp.exp, tiles(log_rate_ref))
    lam = each(lambda v: jnp.exp(-v), rate)
    lam_block = each(lambda v: jnp.exp(v * (-float(SUB))), rate)
    res = tiles(residue_ref)
    sub = lax.broadcasted_iota(jnp.int32, (SUB, LANES), 0)

    def block(i, carry):
        p, w = carry
        index = BLOCKS - 1 - i
        base = pl.multiple_of(index * SUB, SUB)
        parts = [[None] * SUB for _ in range(HALVES)]
        near, near_w = None, None
        far, far_w = p, w
        for k in reversed(range(SUB)):
            rows = [row(g_ref, base + k, h) for h in range(HALVES)]
            p = [[lam[g][h] * p[g][h] + rows[h] for h in range(HALVES)] for g in range(GROUPS)]
            for h in range(HALVES):
                parts[h][k] = res[0][h] * p[0][h] + res[1][h] * p[1][h]
            if near is None:
                near = [rows, rows]
            else:
                a = each(lambda l, v: l * v, lam, near)
                if near_w is None:
                    near_w = a
                else:
                    near_w = each(lambda l, v, c: l * v + c, lam, near_w, a)
                near = [[a[g][h] + rows[h] for h in range(HALVES)] for g in range(GROUPS)]
        w = each(
            lambda n, l, v, q: n + l * (v + float(SUB) * q), near_w, lam_block, far_w, far
        )
        start = pl.multiple_of(index * (MODES * HALVES), SUB)
        for g in range(GROUPS):
            for h in range(HALVES):
                at = tile_rows(start, g, h)
                across_ref[at, :] = lam[g][h] * near[g][h]
                across_lag_ref[at, :] = lam[g][h] * (near_w[g][h] + near[g][h])
        for h in range(HALVES):
            local_ref[span(base, SUB, h)] = fold_sublanes(parts[h])
            own = g_ref[span(base, SUB, h)]
            for d in range(1, SUB):
                moved = jnp.where(sub < SUB - d, pltpu.roll(own, SUB - d, 0), 0.0)
                lagged_ref[pl.ds((d - 1) * HALVES * ROWS + h * ROWS + base, SUB), :] = moved
        return p, w

    p, w = lax.fori_loop(0, BLOCKS, block, (zeros_tiles(), zeros_tiles()))
    for g in range(GROUPS):
        for h in range(HALVES):
            p_ref[g * SUB : (g + 1) * SUB, lane(h)] = p[g][h]
            w_ref[g * SUB : (g + 1) * SUB, lane(h)] = w[g][h]
            rate_ref[tile_rows(0, g, h), :] = rate[g][h]
            weight_ref[tile_rows(0, g, h), :] = res[g][h]
    for g in range(GROUPS):
        for h in range(HALVES):
            for m in range(SUB):
                at = (g * HALVES + h) * SUB + m
                own_rate = rate_ref[pl.ds(at, SUB, stride=0), :]
                own_weight = weight_ref[pl.ds(at, SUB, stride=0), :]
                for k in range(SPAN // SUB):
                    power = (sub + (k * SUB - SPAN)).astype(f32)
                    fade_ref[pl.ds(at * SPAN + k * SUB, SUB), :] = own_weight * jnp.exp(
                        own_rate * power
                    )


def state_kernel(
    recv_ref,
    stream_ref,
    key_ref,
    gain_ref,
    g_ref,
    local_ref,
    p_ref,
    w_ref,
    across_ref,
    across_lag_ref,
    lagged_ref,
    log_rate_ref,
    send_ref,
    x_ref,
    unit_ref,
    inv_ref,
    full_ref,
    u_ref,
):
    total = jnp.sum(recv_ref[...], axis=0)
    inverse = columns(lax.rsqrt(total / D + epsilon))
    gain = gain_ref[...]
    for k in range(4):
        part = pl.ds(k * LANES, LANES)
        inv = jnp.broadcast_to(inverse[k], (LANES, LANES))
        inv_ref[part, :] = inv
        for h in range(HALVES):
            unit = stream_ref[part, lane(h)].astype(f32) * inv
            key = key_ref[part, lane(h)].astype(f32)
            own = span(k * LANES, LANES, h)
            unit_ref[own] = unit
            u_ref[own] = key * unit
            signal = key * (unit * gain[:, lane_slice(h)])
            full_ref[own] = signal
            x_ref[own] = signal.astype(bf16).astype(f32)
    lam = each(lambda v: jnp.exp(-jnp.exp(v)), tiles(log_rate_ref))

    def block(i, carry):
        state, moment, plain, first, second = carry
        base = pl.multiple_of(i * SUB, SUB)
        start = pl.multiple_of(i * (MODES * HALVES), SUB)
        near = [[across_ref[tile_rows(start, g, h), :] for h in range(HALVES)] for g in range(GROUPS)]
        near_lag = [
            [across_lag_ref[tile_rows(start, g, h), :] for h in range(HALVES)]
            for g in range(GROUPS)
        ]
        first = each(lambda f, s, n: f + s * n, first, state, near)
        second = each(
            lambda f, s, n, m, v: f + (s * n + m * v), second, state, near_lag, moment, near
        )
        for k in range(SUB):
            xs = [row(x_ref, base + k, h) for h in range(HALVES)]
            us = [row(u_ref, base + k, h) for h in range(HALVES)]
            a = each(lambda l, v: l * v, lam, state)
            moment = each(lambda l, v, c: l * v + c, lam, moment, a)
            state = [[a[g][h] + xs[h] for h in range(HALVES)] for g in range(GROUPS)]
            plain = [
                [lam[g][h] * plain[g][h] + us[h] for h in range(HALVES)] for g in range(GROUPS)
            ]
        return state, moment, plain, first, second

    zero = zeros_tiles
    start = (zero(), zero(), zero(), zero(), zero())
    state, moment, plain, first, second = lax.fori_loop(0, BLOCKS, block, start)

    def inside(i, carry):
        sums, gains = carry
        base = pl.multiple_of(i * SUB, SUB)
        new_sums, new_gains = [], []
        for h in range(HALVES):
            at = span(base, SUB, h)
            x = x_ref[at]
            new_gains.append(gains[h] + u_ref[at] * local_ref[at])
            own = [sums[h][0] + x * g_ref[at]]
            for d in range(1, SUB):
                moved = lagged_ref[pl.ds((d - 1) * HALVES * ROWS + h * ROWS + base, SUB), :]
                own.append(sums[h][d] + x * moved)
            new_sums.append(own)
        return new_sums, new_gains

    none = jnp.zeros((SUB, LANES), f32)
    sums, gains = lax.fori_loop(
        0, BLOCKS, inside, ([[none] * SUB for _ in range(HALVES)], [none] * HALVES), unroll=2
    )
    near, near_lag = zero(), zero()
    for d in reversed(range(SUB)):
        each_sum = [
            jnp.broadcast_to(jnp.sum(sums[h][d], axis=0, keepdims=True), (SUB, LANES))
            for h in range(HALVES)
        ]
        a = each(lambda l, v: l * v, lam, near)
        near_lag = each(lambda l, v, c: l * v + c, lam, near_lag, a)
        near = [[a[g][h] + each_sum[h] for h in range(HALVES)] for g in range(GROUPS)]
    first = each(lambda f, n: f + n, first, near)
    second = each(lambda f, n: f + n, second, near_lag)
    last = [gains, [jnp.zeros((SUB, LANES), f32)] * HALVES]
    sent = [state, plain, moment, tiles(p_ref), tiles(w_ref), first, second, last]
    for q in range(SUB):
        for g in range(GROUPS):
            for h in range(HALVES):
                at = g * SUB * HALVES * SUB + h * SUB + q
                send_ref[pl.ds(at, SUB, stride=HALVES * SUB), :] = sent[q][g][h]


def shifted(value, k):
    index = lax.broadcasted_iota(jnp.int32, (CHUNKS, LANES), 0)
    return jnp.where(index >= k, pltpu.roll(value, k, 0), 0.0)


def shifted_back(value, k):
    index = lax.broadcasted_iota(jnp.int32, (CHUNKS, LANES), 0)
    return jnp.where(index < CHUNKS - k, pltpu.roll(value, CHUNKS - k, 0), 0.0)


def owner_kernel(recv_ref, log_rate_ref, residue_ref, send_ref):
    state, plain, moment, p, w, first, second, gains = (
        recv_ref[pl.ds(q, CHUNKS, stride=SUB), :] for q in range(SUB)
    )
    rate = jnp.exp(log_rate_ref[...])
    res = residue_ref[...]
    lam = jnp.exp(-rate)
    whole, whole_u, whole_q, back = state, plain, moment, p
    for step in (1, 2, 4, 8, 16):
        far = jnp.exp(rate * (-float(ROWS * step)))
        before = shifted(whole, step)
        whole_q = whole_q + far * (shifted(whole_q, step) + float(ROWS * step) * before)
        whole = whole + far * before
        whole_u = whole_u + far * shifted(whole_u, step)
        back = back + far * shifted_back(back, step)
    into, into_u, into_q = shifted(whole, 1), shifted(whole_u, 1), shifted(whole_q, 1)
    into_p = shifted_back(back, 1)
    scale = 1.0 / math.sqrt(ROWS * CHUNKS)
    grad_residue = jnp.sum(first + lam * (into * p), axis=0, keepdims=True)
    weighted = jnp.sum(second + lam * ((w + p) * into + p * into_q), axis=0, keepdims=True)
    grad_gain = jnp.sum(gains + res * (lam * (into_u * p)), axis=0, keepdims=True)
    shape = (CHUNKS, LANES)
    rows = [
        into,
        into_p,
        jnp.broadcast_to(grad_residue * scale, shape),
        jnp.broadcast_to(-rate * res * weighted * scale, shape),
        jnp.broadcast_to(grad_gain * scale, shape),
    ]
    rows += [jnp.zeros(shape, f32)] * (SUB - len(rows))
    for q in range(SUB):
        send_ref[pl.ds(q, CHUNKS, stride=SUB), :] = rows[q]


def received(ref, q):
    stride = HALVES * SUB
    return [
        [
            ref[pl.ds(g * SUB * stride + h * SUB + q, SUB, stride=stride), :]
            for h in range(HALVES)
        ]
        for g in range(GROUPS)
    ]


def correct_kernel(
    recv_ref,
    local_ref,
    full_ref,
    fade_ref,
    log_rate_ref,
    send_ref,
    total_ref,
    into_ref,
):
    into = received(recv_ref, 1)
    step = each(lambda v: jnp.exp(jnp.exp(v) * (-float(SPAN))), tiles(log_rate_ref))
    spans = ROWS // SPAN
    for b in reversed(range(spans)):
        for g in range(GROUPS):
            for h in range(HALVES):
                into_ref[tile_rows(b * MODES * HALVES, g, h), :] = into[g][h]
        into = each(lambda l, v: l * v, step, into)

    def block(b, carry):
        for h in range(HALVES):
            places = [(g * HALVES + h) * SUB + m for g in range(GROUPS) for m in range(SUB)]
            rows = [into_ref[pl.ds(b * MODES * HALVES + at, SUB, stride=0), :] for at in places]
            for k in range(SPAN // SUB):
                own = span(pl.multiple_of(b * SPAN + k * SUB, SUB), SUB, h)
                terms = [
                    fade_ref[pl.ds(at * SPAN + k * SUB, SUB), :] * rows[m]
                    for m, at in enumerate(places)
                ]
                while len(terms) > 1:
                    terms = [a + b for a, b in zip(terms[::2], terms[1::2])]
                total_ref[own] = local_ref[own] + terms[0]
        return carry

    lax.fori_loop(0, spans, block, 0)
    products = [total_ref[span(0, ROWS, h)] * full_ref[span(0, ROWS, h)] for h in range(HALVES)]
    send_rows(send_ref, sum(products))


def forward_kernel(
    recv_ref,
    x_ref,
    unit_ref,
    inv_ref,
    total_ref,
    key_ref,
    query_ref,
    grad_ref,
    gain_ref,
    log_rate_ref,
    residue_ref,
    output_ref,
    grad_key_ref,
    grad_query_ref,
    left_ref,
    right_ref,
    grad_residue_ref,
    grad_rate_ref,
    grad_gain_ref,
    conv_ref,
):
    lam = each(lambda v: jnp.exp(-jnp.exp(v)), tiles(log_rate_ref))
    res = tiles(residue_ref)

    def block(i, state):
        base = pl.multiple_of(i * SUB, SUB)
        parts = [[None] * SUB for _ in range(HALVES)]
        for k in range(SUB):
            xs = [row(x_ref, base + k, h) for h in range(HALVES)]
            state = [
                [lam[g][h] * state[g][h] + xs[h] for h in range(HALVES)] for g in range(GROUPS)
            ]
            for h in range(HALVES):
                parts[h][k] = res[0][h] * state[0][h] + res[1][h] * state[1][h]
        for h in range(HALVES):
            conv_ref[span(base, SUB, h)] = fold_sublanes(parts[h])
        return state

    lax.fori_loop(0, BLOCKS, block, received(recv_ref, 0))
    gain = gain_ref[...]
    for k in range(4):
        part = pl.ds(k * LANES, LANES)
        inv = inv_ref[part, :]
        for h in range(HALVES):
            at = (part, lane(h))
            own = span(k * LANES, LANES, h)
            conv = conv_ref[own]
            output_ref[at] = (query_ref[at].astype(f32) * conv).astype(bf16)
            grad_query_ref[at] = (grad_ref[at].astype(f32) * conv).astype(bf16)
            unit = unit_ref[own]
            total = total_ref[own]
            own_gain = gain[:, lane_slice(h)]
            grad_key_ref[at] = (total * (unit * own_gain)).astype(bf16)
            left_ref[own] = inv * (total * key_ref[at].astype(f32) * own_gain)
            right_ref[own] = inv * unit
    for q, ref in ((2, grad_residue_ref), (3, grad_rate_ref)):
        found = received(recv_ref, q)
        for g in range(GROUPS):
            for h in range(HALVES):
                ref[g * SUB : (g + 1) * SUB, lane(h)] = found[g][h]
    found = received(recv_ref, 4)
    for h in range(HALVES):
        grad_gain_ref[:, lane(h)] = jnp.sum(found[0][h] + found[1][h], axis=0, keepdims=True)


def finish_kernel(recv_ref, left_ref, right_ref, grad_stream_ref):
    inner = columns(jnp.sum(recv_ref[...], axis=0) / D)
    for k in range(4):
        part = pl.ds(k * LANES, LANES)
        across = jnp.broadcast_to(inner[k], (LANES, LANES))
        for h in range(HALVES):
            own = span(k * LANES, LANES, h)
            value = left_ref[own] - right_ref[own] * across
            grad_stream_ref[part, lane(h)] = value.astype(bf16)


def exchange(value, axis):
    return lax.all_to_all(value, axis, split_axis=0, concat_axis=0, tiled=True)


def local(stream, key_gate, query_gate, grad_output, norm_gain, residue, log_rate):
    wide = (ROWS, COLS)
    split = (HALVES * ROWS, LANES)
    modes = (MODES, COLS)
    tile = (CH, SUB, LANES)
    packed = (CHUNKS * SUB, LANES)
    (squares,) = call(square_kernel, 1, [(tile, f32)], name="square")(stream)
    squares = exchange(squares, "ch")
    log_rate_t = log_rate.T
    residue_t = residue.T
    gain = norm_gain[None, :]
    me = lax.axis_index("ctx")
    log_rate_own = lax.dynamic_slice_in_dim(log_rate_t.reshape(CHUNKS, LANES), me, 1, 0)
    residue_own = lax.dynamic_slice_in_dim(residue_t.reshape(CHUNKS, LANES), me, 1, 0)
    table = (BLOCKS * MODES * HALVES, LANES)
    few = (MODES * HALVES, LANES)
    grad_conv, local_grad, p, w, across, across_lag, lagged, fade = call(
        adjoint_kernel,
        4,
        [
            (split, f32),
            (split, f32),
            (modes, f32),
            (modes, f32),
            (table, f32),
            (table, f32),
            (((SUB - 1) * HALVES * ROWS, LANES), f32),
            ((MODES * HALVES * SPAN, LANES), f32),
        ],
        [pltpu.VMEM(few, f32), pltpu.VMEM(few, f32)],
        name="adjoint",
    )(query_gate, grad_output, log_rate_t, residue_t)
    sent, signal, unit, inv, full = call(
        state_kernel,
        12,
        [(packed, f32), (split, f32), (split, f32), ((ROWS, LANES), f32), (split, f32)],
        [pltpu.VMEM(split, f32)],
        name="state",
    )(
        squares,
        stream,
        key_gate,
        gain,
        grad_conv,
        local_grad,
        p,
        w,
        across,
        across_lag,
        lagged,
        log_rate_t,
    )
    got = exchange(sent.reshape(CHUNKS, SUB, LANES), "ctx").reshape(packed)
    (sent,) = call(owner_kernel, 3, [(packed, f32)], name="owner")(got, log_rate_own, residue_own)
    got = exchange(sent.reshape(CHUNKS, SUB, LANES), "ctx").reshape(packed)
    inner, total = call(
        correct_kernel,
        5,
        [(tile, f32), (split, f32)],
        [pltpu.VMEM((ROWS // SPAN * MODES * HALVES, LANES), f32)],
        name="correct",
    )(got, local_grad, full, fade, log_rate_t)
    inner = exchange(inner, "ch")
    output, grad_key, grad_query, left, right, grad_residue, grad_rate, grad_gain = call(
        forward_kernel,
        11,
        [
            (wide, bf16),
            (wide, bf16),
            (wide, bf16),
            (split, f32),
            (split, f32),
            (modes, f32),
            (modes, f32),
            ((1, COLS), f32),
        ],
        [pltpu.VMEM(split, f32)],
        name="forward",
    )(
        got,
        signal,
        unit,
        inv,
        total,
        key_gate,
        query_gate,
        grad_output,
        gain,
        log_rate_t,
        residue_t,
    )
    (grad_stream,) = call(finish_kernel, 3, [(wide, bf16)], name="finish")(inner, left, right)
    return (
        output,
        grad_stream,
        grad_key,
        grad_query,
        grad_gain[0],
        grad_residue.T,
        grad_rate.T,
    )


def solution(mesh):
    placed = (
        P("ctx", "ch"),
        P("ctx", "ch"),
        P("ctx", "ch"),
        P("ctx", "ch"),
        P("ch"),
        P("ch", None),
        P("ch", None),
    )
    return jax.shard_map(
        local,
        mesh=mesh,
        in_specs=placed,
        out_specs=(
            P("ctx", "ch"),
            P("ctx", "ch"),
            P("ctx", "ch"),
            P("ctx", "ch"),
            P("ch"),
            P("ch", None),
            P("ch", None),
        ),
        check_vma=False,
    )
```

```python
import math

import jax
import jax.numpy as jnp
from jax import lax
from jax.experimental import pallas as pl
from jax.experimental.pallas import tpu as pltpu
from jax.sharding import PartitionSpec as P

D = 4096
MODES = 16
ROWS = 512
COLS = 256
CHUNKS = 32
CH = 16
LANES = 128
SUB = 8
BLOCKS = ROWS // SUB
SPAN = 32
HALVES = COLS // LANES
GROUPS = MODES // SUB
epsilon = 1e-05
f32 = jnp.float32
bf16 = jnp.bfloat16


def call(kernel, ins, outs, scratch=(), limit=8, flops=1 << 22, name=None):
    held = {"v": pl.BlockSpec(memory_space=pltpu.VMEM), "a": pl.BlockSpec(memory_space=pltpu.HBM)}
    return pl.pallas_call(
        kernel,
        in_specs=[held[k] for k in ins],
        out_specs=tuple(held[k] for _, _, k in outs),
        out_shape=tuple(
            pltpu.HBM(s, d) if k == "a" else jax.ShapeDtypeStruct(s, d) for s, d, k in outs
        ),
        scratch_shapes=list(scratch),
        compiler_params=pltpu.CompilerParams(vmem_limit_bytes=limit << 20),
        cost_estimate=pl.CostEstimate(flops=flops, bytes_accessed=1 << 21, transcendentals=0),
        name=name,
    )


def lane(half):
    return pl.ds(half * LANES, LANES)


def lane_slice(half):
    return slice(half * LANES, (half + 1) * LANES)


def tiles(ref):
    return [[ref[g * SUB : (g + 1) * SUB, lane(h)] for h in range(HALVES)] for g in range(GROUPS)]


def each(fn, *args):
    return [[fn(*(a[g][h] for a in args)) for h in range(HALVES)] for g in range(GROUPS)]


def zeros_tiles():
    return [[jnp.zeros((SUB, LANES), f32) for _ in range(HALVES)] for _ in range(GROUPS)]


def fold_sublanes(parts):
    sub = lax.broadcasted_iota(jnp.int32, (SUB, LANES), 0)
    low4 = sub < 4
    low2 = (sub & 2) == 0
    low1 = (sub & 1) == 0
    four = []
    for k in range(4):
        a, b = parts[k], parts[k + 4]
        four.append(jnp.where(low4, a, b) + pltpu.roll(jnp.where(low4, b, a), 4, 0))
    two = []
    for k in range(2):
        a, b = four[k], four[k + 2]
        two.append(jnp.where(low2, a + pltpu.roll(a, 6, 0), b + pltpu.roll(b, 2, 0)))
    a, b = two
    return jnp.where(low1, a + pltpu.roll(a, 7, 0), b + pltpu.roll(b, 1, 0))


def row(ref, t, half):
    return ref[pl.ds(half * ROWS + t, SUB, stride=0), :]


def span(start, size, half):
    return (pl.ds(half * ROWS + start, size), slice(None))


def send_rows(ref, values):
    sub = lax.broadcasted_iota(jnp.int32, (SUB, LANES), 0) & 3
    tile = None
    for k in range(4):
        turned = values[k * LANES : (k + 1) * LANES].T
        part = jnp.broadcast_to(jnp.sum(turned, axis=0, keepdims=True), (SUB, LANES))
        tile = part if tile is None else jnp.where(sub == k, part, tile)
    ref[...] = jnp.broadcast_to(tile[None], (CH, SUB, LANES))


def columns(tile):
    turned = tile.T
    return [turned[:, k : k + 1] for k in range(4)]


def square_kernel(stream_ref, send_ref):
    wide = [stream_ref[:, lane(h)].astype(f32) for h in range(HALVES)]
    send_rows(send_ref, sum(v * v for v in wide))


def tile_rows(start, group, half):
    return pl.ds(start + (group * HALVES + half) * SUB, SUB)


def adjoint_kernel(
    query_ref,
    grad_ref,
    log_rate_ref,
    residue_ref,
    gain_ref,
    g_ref,
    local_out,
    p_ref,
    w_ref,
    across_ref,
    across_lag_ref,
    gain_out,
    local_ref,
    done,
):
    gain_out[...] = gain_ref[...]
    for h in range(HALVES):
        g_ref[span(0, ROWS, h)] = grad_ref[:, lane(h)].astype(f32) * query_ref[
            :, lane(h)
        ].astype(f32)
    rate = each(jnp.exp, tiles(log_rate_ref))
    lam = each(lambda v: jnp.exp(-v), rate)
    lam_block = each(lambda v: jnp.exp(v * (-float(SUB))), rate)
    res = tiles(residue_ref)

    def block(i, carry):
        p, w = carry
        index = BLOCKS - 1 - i
        base = pl.multiple_of(index * SUB, SUB)
        parts = [[None] * SUB for _ in range(HALVES)]
        near, near_w = None, None
        far, far_w = p, w
        for k in reversed(range(SUB)):
            rows = [row(g_ref, base + k, h) for h in range(HALVES)]
            p = [[lam[g][h] * p[g][h] + rows[h] for h in range(HALVES)] for g in range(GROUPS)]
            for h in range(HALVES):
                parts[h][k] = res[0][h] * p[0][h] + res[1][h] * p[1][h]
            if near is None:
                near = [rows, rows]
            else:
                a = each(lambda l, v: l * v, lam, near)
                if near_w is None:
                    near_w = a
                else:
                    near_w = each(lambda l, v, c: l * v + c, lam, near_w, a)
                near = [[a[g][h] + rows[h] for h in range(HALVES)] for g in range(GROUPS)]
        w = each(
            lambda n, l, v, q: n + l * (v + float(SUB) * q), near_w, lam_block, far_w, far
        )
        start = pl.multiple_of(index * (MODES * HALVES), SUB)
        for g in range(GROUPS):
            for h in range(HALVES):
                at = tile_rows(start, g, h)
                across_ref[at, :] = lam[g][h] * near[g][h]
                across_lag_ref[at, :] = lam[g][h] * (near_w[g][h] + near[g][h])
        for h in range(HALVES):
            local_ref[span(base, SUB, h)] = fold_sublanes(parts[h])
        return p, w

    p, w = lax.fori_loop(0, BLOCKS, block, (zeros_tiles(), zeros_tiles()))
    copy = pltpu.make_async_copy(local_ref, local_out, done)
    copy.start()
    for g in range(GROUPS):
        for h in range(HALVES):
            p_ref[g * SUB : (g + 1) * SUB, lane(h)] = p[g][h]
            w_ref[g * SUB : (g + 1) * SUB, lane(h)] = w[g][h]
    copy.wait()


def fade_kernel(log_rate_ref, residue_ref, after_ref, fade_ref, rate_ref, weight_ref):
    sub = lax.broadcasted_iota(jnp.int32, (SUB, LANES), 0)
    rate = each(jnp.exp, tiles(log_rate_ref))
    res = tiles(residue_ref)
    for g in range(GROUPS):
        for h in range(HALVES):
            rate_ref[tile_rows(0, g, h), :] = rate[g][h]
            weight_ref[tile_rows(0, g, h), :] = res[g][h]

    def block(at, carry):
        own_rate = rate_ref[pl.ds(at, SUB, stride=0), :]
        own_weight = weight_ref[pl.ds(at, SUB, stride=0), :]
        for k in range(SPAN // SUB):
            power = (sub + (k * SUB - SPAN)).astype(f32)
            rows = pl.ds(pl.multiple_of(at * SPAN + k * SUB, SUB), SUB)
            fade_ref[rows, :] = own_weight * jnp.exp(own_rate * power)
        return carry

    lax.fori_loop(0, MODES * HALVES, block, 0, unroll=4)


def state_kernel(
    recv_ref,
    stream_ref,
    key_ref,
    gain_ref,
    g_ref,
    local_in,
    p_ref,
    w_ref,
    across_ref,
    across_lag_ref,
    log_rate_ref,
    send_out,
    signal_out,
    inv_out,
    full_out,
    send_ref,
    signal_ref,
    inv_ref,
    full_ref,
    local_ref,
    x_ref,
    u_ref,
    done,
):
    fetch = pltpu.make_async_copy(local_in, local_ref, done.at[0])
    fetch.start()
    total = jnp.sum(recv_ref[...], axis=0)
    inverse = columns(lax.rsqrt(total / D + epsilon))
    gain = gain_ref[...]
    for k in range(4):
        part = pl.ds(k * LANES, LANES)
        inv = jnp.broadcast_to(inverse[k], (LANES, LANES))
        inv_ref[part, :] = inv
        for h in range(HALVES):
            unit = stream_ref[part, lane(h)].astype(f32) * inv
            key = key_ref[part, lane(h)].astype(f32)
            own = span(k * LANES, LANES, h)
            u_ref[own] = key * unit
            signal = key * (unit * gain[:, lane_slice(h)])
            full_ref[own] = signal
            narrow = signal.astype(bf16)
            signal_ref[own] = narrow
            x_ref[own] = narrow.astype(f32)
    stores = [
        pltpu.make_async_copy(signal_ref, signal_out, done.at[1]),
        pltpu.make_async_copy(inv_ref, inv_out, done.at[2]),
        pltpu.make_async_copy(full_ref, full_out, done.at[3]),
    ]
    for copy in stores:
        copy.start()
    lam = each(lambda v: jnp.exp(-jnp.exp(v)), tiles(log_rate_ref))

    def block(i, carry):
        state, moment, plain, first, second = carry
        base = pl.multiple_of(i * SUB, SUB)
        start = pl.multiple_of(i * (MODES * HALVES), SUB)
        near = [[across_ref[tile_rows(start, g, h), :] for h in range(HALVES)] for g in range(GROUPS)]
        near_lag = [
            [across_lag_ref[tile_rows(start, g, h), :] for h in range(HALVES)]
            for g in range(GROUPS)
        ]
        first = each(lambda f, s, n: f + s * n, first, state, near)
        second = each(
            lambda f, s, n, m, v: f + (s * n + m * v), second, state, near_lag, moment, near
        )
        for k in range(SUB):
            xs = [row(x_ref, base + k, h) for h in range(HALVES)]
            us = [row(u_ref, base + k, h) for h in range(HALVES)]
            a = each(lambda l, v: l * v, lam, state)
            moment = each(lambda l, v, c: l * v + c, lam, moment, a)
            state = [[a[g][h] + xs[h] for h in range(HALVES)] for g in range(GROUPS)]
            plain = [
                [lam[g][h] * plain[g][h] + us[h] for h in range(HALVES)] for g in range(GROUPS)
            ]
        return state, moment, plain, first, second

    zero = zeros_tiles
    start = (zero(), zero(), zero(), zero(), zero())
    state, moment, plain, first, second = lax.fori_loop(0, BLOCKS, block, start)

    sub = lax.broadcasted_iota(jnp.int32, (SUB, LANES), 0)

    def inside(i, carry):
        sums, gains = carry
        base = pl.multiple_of(i * SUB, SUB)
        new_sums, new_gains = [], []
        for h in range(HALVES):
            at = span(base, SUB, h)
            x = x_ref[at]
            new_gains.append(gains[h] + u_ref[at] * local_ref[at])
            later = g_ref[at]
            own = [sums[h][0] + x * later]
            for d in range(1, SUB):
                moved = jnp.where(sub < SUB - d, pltpu.roll(later, SUB - d, 0), 0.0)
                own.append(sums[h][d] + x * moved)
            new_sums.append(own)
        return new_sums, new_gains

    fetch.wait()
    none = jnp.zeros((SUB, LANES), f32)
    sums, gains = lax.fori_loop(
        0, BLOCKS, inside, ([[none] * SUB for _ in range(HALVES)], [none] * HALVES), unroll=2
    )
    near, near_lag = zero(), zero()
    for d in reversed(range(SUB)):
        each_sum = [
            jnp.broadcast_to(jnp.sum(sums[h][d], axis=0, keepdims=True), (SUB, LANES))
            for h in range(HALVES)
        ]
        a = each(lambda l, v: l * v, lam, near)
        near_lag = each(lambda l, v, c: l * v + c, lam, near_lag, a)
        near = [[a[g][h] + each_sum[h] for h in range(HALVES)] for g in range(GROUPS)]
    first = each(lambda f, n: f + n, first, near)
    second = each(lambda f, n: f + n, second, near_lag)
    last = [gains, [jnp.zeros((SUB, LANES), f32)] * HALVES]
    sent = [state, plain, moment, tiles(p_ref), tiles(w_ref), first, second, last]
    flat_ref = send_ref.reshape(CHUNKS * SUB, LANES)
    for q in range(SUB):
        for g in range(GROUPS):
            for h in range(HALVES):
                at = g * SUB * HALVES * SUB + h * SUB + q
                flat_ref[pl.ds(at, SUB, stride=HALVES * SUB), :] = sent[q][g][h]
    copy = pltpu.make_async_copy(send_ref, send_out, done.at[4])
    copy.start()
    for store in stores:
        store.wait()
    copy.wait()


def shifted(value, k):
    index = lax.broadcasted_iota(jnp.int32, (CHUNKS, LANES), 0)
    return jnp.where(index >= k, pltpu.roll(value, k, 0), 0.0)


def shifted_back(value, k):
    index = lax.broadcasted_iota(jnp.int32, (CHUNKS, LANES), 0)
    return jnp.where(index < CHUNKS - k, pltpu.roll(value, CHUNKS - k, 0), 0.0)


def owner_kernel(recv_ref, log_rate_ref, residue_ref, send_ref):
    flat_ref = recv_ref.reshape(CHUNKS * SUB, LANES)
    state, plain, moment, p, w, first, second, gains = (
        flat_ref[pl.ds(q, CHUNKS, stride=SUB), :] for q in range(SUB)
    )
    rate = jnp.exp(log_rate_ref[...])
    res = residue_ref[...]
    lam = jnp.exp(-rate)
    whole, whole_u, whole_q, back = state, plain, moment, p
    for step in (1, 2, 4, 8, 16):
        far = jnp.exp(rate * (-float(ROWS * step)))
        before = shifted(whole, step)
        whole_q = whole_q + far * (shifted(whole_q, step) + float(ROWS * step) * before)
        whole = whole + far * before
        whole_u = whole_u + far * shifted(whole_u, step)
        back = back + far * shifted_back(back, step)
    into, into_u, into_q = shifted(whole, 1), shifted(whole_u, 1), shifted(whole_q, 1)
    into_p = shifted_back(back, 1)
    scale = 1.0 / math.sqrt(ROWS * CHUNKS)
    grad_residue = jnp.sum(first + lam * (into * p), axis=0, keepdims=True)
    weighted = jnp.sum(second + lam * ((w + p) * into + p * into_q), axis=0, keepdims=True)
    grad_gain = jnp.sum(gains + res * (lam * (into_u * p)), axis=0, keepdims=True)
    shape = (CHUNKS, LANES)
    rows = [
        into,
        into_p,
        jnp.broadcast_to(grad_residue * scale, shape),
        jnp.broadcast_to(-rate * res * weighted * scale, shape),
        jnp.broadcast_to(grad_gain * scale, shape),
    ]
    rows += [jnp.zeros(shape, f32)] * (SUB - len(rows))
    flat_ref = send_ref.reshape(CHUNKS * SUB, LANES)
    for q in range(SUB):
        flat_ref[pl.ds(q, CHUNKS, stride=SUB), :] = rows[q]


def received(ref, q):
    stride = HALVES * SUB
    flat_ref = ref.reshape(CHUNKS * SUB, LANES)
    return [
        [
            flat_ref[pl.ds(g * SUB * stride + h * SUB + q, SUB, stride=stride), :]
            for h in range(HALVES)
        ]
        for g in range(GROUPS)
    ]


def correct_kernel(
    recv_ref,
    local_ref,
    full_ref,
    fade_ref,
    log_rate_ref,
    send_ref,
    total_out,
    into_ref,
    total_ref,
    done,
):
    into = received(recv_ref, 1)
    step = each(lambda v: jnp.exp(jnp.exp(v) * (-float(SPAN))), tiles(log_rate_ref))
    spans = ROWS // SPAN
    for b in reversed(range(spans)):
        for g in range(GROUPS):
            for h in range(HALVES):
                into_ref[tile_rows(b * MODES * HALVES, g, h), :] = into[g][h]
        into = each(lambda l, v: l * v, step, into)

    def block(b, carry):
        for h in range(HALVES):
            places = [(g * HALVES + h) * SUB + m for g in range(GROUPS) for m in range(SUB)]
            rows = [into_ref[pl.ds(b * MODES * HALVES + at, SUB, stride=0), :] for at in places]
            for k in range(SPAN // SUB):
                own = span(pl.multiple_of(b * SPAN + k * SUB, SUB), SUB, h)
                terms = [
                    fade_ref[pl.ds(at * SPAN + k * SUB, SUB), :] * rows[m]
                    for m, at in enumerate(places)
                ]
                while len(terms) > 1:
                    terms = [a + b for a, b in zip(terms[::2], terms[1::2])]
                total_ref[own] = local_ref[own] + terms[0]
        return carry

    lax.fori_loop(0, spans, block, 0)
    copy = pltpu.make_async_copy(total_ref, total_out, done)
    copy.start()
    products = [total_ref[span(0, ROWS, h)] * full_ref[span(0, ROWS, h)] for h in range(HALVES)]
    send_rows(send_ref, sum(products))
    copy.wait()


def forward_kernel(
    recv_ref,
    signal_ref,
    inv_ref,
    total_ref,
    stream_ref,
    key_ref,
    query_ref,
    grad_ref,
    gain_ref,
    log_rate_ref,
    residue_ref,
    output_ref,
    grad_key_ref,
    grad_query_ref,
    left_ref,
    right_ref,
    grad_residue_ref,
    grad_rate_ref,
    grad_gain_ref,
    conv_ref,
    x_ref,
):
    x_ref[...] = signal_ref[...].astype(f32)
    lam = each(lambda v: jnp.exp(-jnp.exp(v)), tiles(log_rate_ref))
    res = tiles(residue_ref)

    def block(i, state):
        base = pl.multiple_of(i * SUB, SUB)
        parts = [[None] * SUB for _ in range(HALVES)]
        for k in range(SUB):
            xs = [row(x_ref, base + k, h) for h in range(HALVES)]
            state = [
                [lam[g][h] * state[g][h] + xs[h] for h in range(HALVES)] for g in range(GROUPS)
            ]
            for h in range(HALVES):
                parts[h][k] = res[0][h] * state[0][h] + res[1][h] * state[1][h]
        for h in range(HALVES):
            conv_ref[span(base, SUB, h)] = fold_sublanes(parts[h])
        return state

    lax.fori_loop(0, BLOCKS, block, received(recv_ref, 0))
    gain = gain_ref[...]
    for k in range(4):
        part = pl.ds(k * LANES, LANES)
        inv = inv_ref[part, :]
        for h in range(HALVES):
            at = (part, lane(h))
            own = span(k * LANES, LANES, h)
            conv = conv_ref[own]
            output_ref[at] = (query_ref[at].astype(f32) * conv).astype(bf16)
            grad_query_ref[at] = (grad_ref[at].astype(f32) * conv).astype(bf16)
            unit = stream_ref[at].astype(f32) * inv
            total = total_ref[own]
            own_gain = gain[:, lane_slice(h)]
            grad_key_ref[at] = (total * (unit * own_gain)).astype(bf16)
            left_ref[own] = inv * (total * key_ref[at].astype(f32) * own_gain)
            right_ref[own] = inv * unit
    for q, ref in ((2, grad_residue_ref), (3, grad_rate_ref)):
        found = received(recv_ref, q)
        for g in range(GROUPS):
            for h in range(HALVES):
                ref[g * SUB : (g + 1) * SUB, lane(h)] = found[g][h]
    found = received(recv_ref, 4)
    for h in range(HALVES):
        grad_gain_ref[:, lane(h)] = jnp.sum(found[0][h] + found[1][h], axis=0, keepdims=True)


def finish_kernel(recv_ref, left_ref, right_ref, grad_stream_ref):
    inner = columns(jnp.sum(recv_ref[...], axis=0) / D)
    for k in range(4):
        part = pl.ds(k * LANES, LANES)
        across = jnp.broadcast_to(inner[k], (LANES, LANES))
        for h in range(HALVES):
            own = span(k * LANES, LANES, h)
            value = left_ref[own] - right_ref[own] * across
            grad_stream_ref[part, lane(h)] = value.astype(bf16)


def in_hbm(value):
    return pltpu.with_memory_space_constraint(value, pltpu.HBM)


def exchange(value, axis):
    return lax.all_to_all(value, axis, split_axis=0, concat_axis=0, tiled=True)


def local(stream, key_gate, query_gate, grad_output, norm_gain, residue, log_rate):
    wide = (ROWS, COLS)
    split = (HALVES * ROWS, LANES)
    modes = (MODES, COLS)
    tile = (CH, SUB, LANES)
    (squares,) = call(square_kernel, "v", [(tile, f32, "v")], name="square")(stream)
    squares = exchange(squares, "ch")
    log_rate_t = log_rate.T
    residue_t = residue.T
    me = lax.axis_index("ctx")
    log_rate_own = lax.dynamic_slice_in_dim(log_rate_t.reshape(CHUNKS, LANES), me, 1, 0)
    residue_own = lax.dynamic_slice_in_dim(residue_t.reshape(CHUNKS, LANES), me, 1, 0)
    table = (BLOCKS * MODES * HALVES, LANES)
    few = (MODES * HALVES, LANES)
    packed = (CHUNKS, SUB, LANES)
    grad_conv, local_grad, p, w, across, across_lag, gain = call(
        adjoint_kernel,
        "vvvvv",
        [
            (split, f32, "v"),
            (split, f32, "a"),
            (modes, f32, "v"),
            (modes, f32, "v"),
            (table, f32, "v"),
            (table, f32, "v"),
            ((1, COLS), f32, "v"),
        ],
        [pltpu.VMEM(split, f32), pltpu.SemaphoreType.DMA],
        name="adjoint",
    )(query_gate, grad_output, log_rate_t, residue_t, norm_gain[None, :])
    rows = (ROWS, LANES)
    sent, signal, inv, full = call(
        state_kernel,
        "vvvvvavvvvv",
        [(packed, f32, "a"), (split, bf16, "a"), (rows, f32, "a"), (split, f32, "a")],
        [
            pltpu.VMEM(packed, f32),
            pltpu.VMEM(split, bf16),
            pltpu.VMEM(rows, f32),
            pltpu.VMEM(split, f32),
            pltpu.VMEM(split, f32),
            pltpu.VMEM(split, f32),
            pltpu.VMEM(split, f32),
            pltpu.SemaphoreType.DMA((5,)),
        ],
        name="state",
    )(
        squares,
        stream,
        key_gate,
        gain,
        grad_conv,
        in_hbm(local_grad),
        p,
        w,
        across,
        across_lag,
        log_rate_t,
    )
    got = exchange(sent, "ctx")
    (fade,) = call(
        fade_kernel,
        "vva",
        [((MODES * HALVES * SPAN, LANES), f32, "v")],
        [pltpu.VMEM(few, f32), pltpu.VMEM(few, f32)],
        name="fade",
    )(log_rate_t, residue_t, in_hbm(inv))
    (sent,) = call(owner_kernel, "vvv", [(packed, f32, "v")], name="owner")(
        got, log_rate_own, residue_own
    )
    got = exchange(sent, "ctx")
    inner, total = call(
        correct_kernel,
        "vvvvv",
        [(tile, f32, "v"), (split, f32, "a")],
        [
            pltpu.VMEM((ROWS // SPAN * MODES * HALVES, LANES), f32),
            pltpu.VMEM(split, f32),
            pltpu.SemaphoreType.DMA,
        ],
        name="correct",
    )(got, local_grad, full, fade, log_rate_t)
    inner = exchange(inner, "ch")
    output, grad_key, grad_query, left, right, grad_residue, grad_rate, grad_gain = call(
        forward_kernel,
        "v" * 11,
        [
            (wide, bf16, "v"),
            (wide, bf16, "v"),
            (wide, bf16, "v"),
            (split, f32, "v"),
            (split, f32, "v"),
            (modes, f32, "v"),
            (modes, f32, "v"),
            ((1, COLS), f32, "v"),
        ],
        [pltpu.VMEM(split, f32), pltpu.VMEM(split, f32)],
        name="forward",
    )(
        got,
        signal,
        inv,
        total,
        stream,
        key_gate,
        query_gate,
        grad_output,
        gain,
        log_rate_t,
        residue_t,
    )
    (grad_stream,) = call(finish_kernel, "vvv", [(wide, bf16, "v")], name="finish")(inner, left, right)
    return (
        output,
        grad_stream,
        grad_key,
        grad_query,
        grad_gain[0],
        grad_residue.T,
        grad_rate.T,
    )


def solution(mesh):
    placed = (
        P("ctx", "ch"),
        P("ctx", "ch"),
        P("ctx", "ch"),
        P("ctx", "ch"),
        P("ch"),
        P("ch", None),
        P("ch", None),
    )
    return jax.shard_map(
        local,
        mesh=mesh,
        in_specs=placed,
        out_specs=(
            P("ctx", "ch"),
            P("ctx", "ch"),
            P("ctx", "ch"),
            P("ctx", "ch"),
            P("ch"),
            P("ch", None),
            P("ch", None),
        ),
        check_vma=False,
    )
```

```python
import math

import jax
import jax.numpy as jnp
from jax import lax
from jax.experimental import pallas as pl
from jax.experimental.pallas import tpu as pltpu
from jax.sharding import PartitionSpec as P

D = 4096
MODES = 16
ROWS = 512
COLS = 256
CHUNKS = 32
CH = 16
LANES = 128
SUB = 8
BLOCKS = ROWS // SUB
SPAN = 16
QUARTERS = ROWS // LANES
HALVES = COLS // LANES
GROUPS = MODES // SUB
epsilon = 1e-05
f32 = jnp.float32
bf16 = jnp.bfloat16


def call(kernel, ins, outs, scratch=(), limit=8, flops=1 << 22, name=None):
    held = {"v": pl.BlockSpec(memory_space=pltpu.VMEM), "a": pl.BlockSpec(memory_space=pltpu.HBM)}
    return pl.pallas_call(
        kernel,
        in_specs=[held[k] for k in ins],
        out_specs=tuple(held[k] for _, _, k in outs),
        out_shape=tuple(
            pltpu.HBM(s, d) if k == "a" else jax.ShapeDtypeStruct(s, d) for s, d, k in outs
        ),
        scratch_shapes=list(scratch),
        compiler_params=pltpu.CompilerParams(vmem_limit_bytes=limit << 20),
        cost_estimate=pl.CostEstimate(flops=flops, bytes_accessed=1 << 21, transcendentals=0),
        name=name,
    )


def lane(half):
    return pl.ds(half * LANES, LANES)


def lane_slice(half):
    return slice(half * LANES, (half + 1) * LANES)


def tiles(ref):
    return [[ref[g * SUB : (g + 1) * SUB, lane(h)] for h in range(HALVES)] for g in range(GROUPS)]


def each(fn, *args):
    return [[fn(*(a[g][h] for a in args)) for h in range(HALVES)] for g in range(GROUPS)]


def zeros_tiles():
    return [[jnp.zeros((SUB, LANES), f32) for _ in range(HALVES)] for _ in range(GROUPS)]


def fold_sublanes(parts):
    sub = lax.broadcasted_iota(jnp.int32, (SUB, LANES), 0)
    low4 = sub < 4
    low2 = (sub & 2) == 0
    low1 = (sub & 1) == 0
    four = []
    for k in range(4):
        a, b = parts[k], parts[k + 4]
        four.append(jnp.where(low4, a, b) + pltpu.roll(jnp.where(low4, b, a), 4, 0))
    two = []
    for k in range(2):
        a, b = four[k], four[k + 2]
        two.append(jnp.where(low2, a + pltpu.roll(a, 6, 0), b + pltpu.roll(b, 2, 0)))
    a, b = two
    return jnp.where(low1, a + pltpu.roll(a, 7, 0), b + pltpu.roll(b, 1, 0))


def row(ref, t, half):
    return ref[pl.ds(half * ROWS + t, SUB, stride=0), :]


def span(start, size, half):
    return (pl.ds(half * ROWS + start, size), slice(None))


def lane_totals(values):
    return jnp.broadcast_to(jnp.sum(values.T, axis=0, keepdims=True), (SUB, LANES))


def send_rows(ref, parts):
    sub = lax.broadcasted_iota(jnp.int32, (SUB, LANES), 0) & 3
    tile = parts[0]
    for k in range(1, QUARTERS):
        tile = jnp.where(sub == k, parts[k], tile)
    ref[...] = jnp.broadcast_to(tile[None], (CH, SUB, LANES))


def columns(tile):
    turned = tile.T
    return [turned[:, k : k + 1] for k in range(4)]


def square_kernel(stream_ref, send_ref):
    parts = []
    for k in range(QUARTERS):
        part = pl.ds(k * LANES, LANES)
        wide = [stream_ref[part, lane(h)].astype(f32) for h in range(HALVES)]
        parts.append(lane_totals(sum(v * v for v in wide)))
    send_rows(send_ref, parts)


def tile_rows(start, group, half):
    return pl.ds(start + (group * HALVES + half) * SUB, SUB)


def adjoint_kernel(
    query_ref,
    grad_ref,
    log_rate_ref,
    residue_ref,
    gain_ref,
    own_log_rate_ref,
    own_residue_ref,
    g_out,
    local_out,
    p_ref,
    w_ref,
    across_ref,
    across_lag_ref,
    gain_out,
    own_log_rate_out,
    own_residue_out,
    g_ref,
    local_ref,
    done,
):
    gain_out[...] = gain_ref[...]
    own_log_rate_out[...] = own_log_rate_ref[...]
    own_residue_out[...] = own_residue_ref[...]
    for h in range(HALVES):
        g_ref[span(0, ROWS, h)] = grad_ref[:, lane(h)].astype(f32) * query_ref[
            :, lane(h)
        ].astype(f32)
    g_copy = pltpu.make_async_copy(
        g_ref.reshape(HALVES * BLOCKS, SUB, LANES), g_out, done.at[1]
    )
    g_copy.start()
    rate = each(jnp.exp, tiles(log_rate_ref))
    lam = each(lambda v: jnp.exp(-v), rate)
    lam_block = each(lambda v: jnp.exp(v * (-float(SUB))), rate)
    res = tiles(residue_ref)

    def block(i, carry):
        p, w = carry
        index = BLOCKS - 1 - i
        base = pl.multiple_of(index * SUB, SUB)
        parts = [[None] * SUB for _ in range(HALVES)]
        near, near_w = None, None
        far, far_w = p, w
        for k in reversed(range(SUB)):
            rows = [row(g_ref, base + k, h) for h in range(HALVES)]
            p = [[lam[g][h] * p[g][h] + rows[h] for h in range(HALVES)] for g in range(GROUPS)]
            for h in range(HALVES):
                parts[h][k] = res[0][h] * p[0][h] + res[1][h] * p[1][h]
            if near is None:
                near = [rows, rows]
            else:
                a = each(lambda l, v: l * v, lam, near)
                if near_w is None:
                    near_w = a
                else:
                    near_w = each(lambda l, v, c: l * v + c, lam, near_w, a)
                near = [[a[g][h] + rows[h] for h in range(HALVES)] for g in range(GROUPS)]
        w = each(
            lambda n, l, v, q: n + l * (v + float(SUB) * q), near_w, lam_block, far_w, far
        )
        start = pl.multiple_of(index * (MODES * HALVES), SUB)
        for g in range(GROUPS):
            for h in range(HALVES):
                at = tile_rows(start, g, h)
                across_ref[at, :] = lam[g][h] * near[g][h]
                across_lag_ref[at, :] = lam[g][h] * (near_w[g][h] + near[g][h])
        for h in range(HALVES):
            local_ref[span(base, SUB, h)] = fold_sublanes(parts[h])
        return p, w

    p, w = lax.fori_loop(0, BLOCKS, block, (zeros_tiles(), zeros_tiles()))
    copy = pltpu.make_async_copy(local_ref, local_out, done.at[0])
    copy.start()
    for g in range(GROUPS):
        for h in range(HALVES):
            p_ref[g * SUB : (g + 1) * SUB, lane(h)] = p[g][h]
            w_ref[g * SUB : (g + 1) * SUB, lane(h)] = w[g][h]
    copy.wait()
    g_copy.wait()


def fill_fade(log_rate_ref, residue_ref, fade_ref, rate_ref, weight_ref):
    sub = lax.broadcasted_iota(jnp.int32, (SUB, LANES), 0)
    rate = each(jnp.exp, tiles(log_rate_ref))
    res = tiles(residue_ref)
    for g in range(GROUPS):
        for h in range(HALVES):
            rate_ref[tile_rows(0, g, h), :] = rate[g][h]
            weight_ref[tile_rows(0, g, h), :] = res[g][h]

    def block(at, carry):
        own_rate = rate_ref[pl.ds(at, SUB, stride=0), :]
        own_weight = weight_ref[pl.ds(at, SUB, stride=0), :]
        for k in range(SPAN // SUB):
            power = (sub + (k * SUB - SPAN)).astype(f32)
            rows = pl.ds(pl.multiple_of(at * SPAN + k * SUB, SUB), SUB)
            fade_ref[rows, :] = own_weight * jnp.exp(own_rate * power)
        return carry

    lax.fori_loop(0, MODES * HALVES, block, 0, unroll=8)


def state_kernel(
    recv_ref,
    stream_ref,
    key_ref,
    gain_ref,
    g_in,
    local_in,
    p_ref,
    w_ref,
    across_ref,
    across_lag_ref,
    log_rate_ref,
    send_ref,
    signal_out,
    inv_out,
    full_ref,
    signal_ref,
    inv_ref,
    local_ref,
    x_ref,
    u_ref,
    padded_ref,
    done,
):
    fetch = pltpu.make_async_copy(local_in, local_ref, done.at[0])
    fetch.start()
    wider_ref = padded_ref.reshape(HALVES * BLOCKS, 2 * SUB, LANES)
    fetch_g = pltpu.make_async_copy(g_in, wider_ref.at[:, pl.ds(0, SUB), :], done.at[3])
    fetch_g.start()
    total = jnp.sum(recv_ref[...], axis=0)
    inverse = columns(lax.rsqrt(total / D + epsilon))
    gain = gain_ref[...]
    for k in range(4):
        part = pl.ds(k * LANES, LANES)
        inv = jnp.broadcast_to(inverse[k], (LANES, LANES))
        inv_ref[part, :] = inv
        for h in range(HALVES):
            unit = stream_ref[part, lane(h)].astype(f32) * inv
            key = key_ref[part, lane(h)].astype(f32)
            own = span(k * LANES, LANES, h)
            u_ref[own] = key * unit
            signal = key * (unit * gain[:, lane_slice(h)])
            full_ref[own] = signal
            narrow = signal.astype(bf16)
            signal_ref[own] = narrow
            x_ref[own] = narrow.astype(f32)
    stores = [
        pltpu.make_async_copy(signal_ref, signal_out, done.at[1]),
        pltpu.make_async_copy(inv_ref, inv_out, done.at[2]),
    ]
    for copy in stores:
        copy.start()
    lam = each(lambda v: jnp.exp(-jnp.exp(v)), tiles(log_rate_ref))

    def block(i, carry):
        state, moment, plain, first, second = carry
        base = pl.multiple_of(i * SUB, SUB)
        start = pl.multiple_of(i * (MODES * HALVES), SUB)
        near = [[across_ref[tile_rows(start, g, h), :] for h in range(HALVES)] for g in range(GROUPS)]
        near_lag = [
            [across_lag_ref[tile_rows(start, g, h), :] for h in range(HALVES)]
            for g in range(GROUPS)
        ]
        first = each(lambda f, s, n: f + s * n, first, state, near)
        second = each(
            lambda f, s, n, m, v: f + (s * n + m * v), second, state, near_lag, moment, near
        )
        for h in range(HALVES):
            wider = pl.multiple_of((h * BLOCKS + i) * 2 * SUB, 2 * SUB)
            padded_ref[pl.ds(wider + SUB, SUB), :] = jnp.zeros((SUB, LANES), f32)
        for k in range(SUB):
            xs = [row(x_ref, base + k, h) for h in range(HALVES)]
            us = [row(u_ref, base + k, h) for h in range(HALVES)]
            a = each(lambda l, v: l * v, lam, state)
            moment = each(lambda l, v, c: l * v + c, lam, moment, a)
            state = [[a[g][h] + xs[h] for h in range(HALVES)] for g in range(GROUPS)]
            plain = [
                [lam[g][h] * plain[g][h] + us[h] for h in range(HALVES)] for g in range(GROUPS)
            ]
        return state, moment, plain, first, second

    zero = zeros_tiles
    start = (zero(), zero(), zero(), zero(), zero())
    state, moment, plain, first, second = lax.fori_loop(0, BLOCKS, block, start)


    def inside(i, carry):
        sums, gains = carry
        base = pl.multiple_of(i * SUB, SUB)
        new_sums, new_gains = [], []
        for h in range(HALVES):
            at = span(base, SUB, h)
            x = x_ref[at]
            new_gains.append(gains[h] + u_ref[at] * local_ref[at])
            wider = pl.multiple_of((h * BLOCKS + i) * 2 * SUB, 2 * SUB)
            own = [
                sums[h][d] + x * padded_ref[pl.ds(wider + d, SUB), :] for d in range(SUB)
            ]
            new_sums.append(own)
        return new_sums, new_gains

    fetch.wait()
    fetch_g.wait()
    none = jnp.zeros((SUB, LANES), f32)
    sums, gains = lax.fori_loop(
        0, BLOCKS, inside, ([[none] * SUB for _ in range(HALVES)], [none] * HALVES), unroll=2
    )
    near, near_lag = zero(), zero()
    for d in reversed(range(SUB)):
        each_sum = [
            jnp.broadcast_to(jnp.sum(sums[h][d], axis=0, keepdims=True), (SUB, LANES))
            for h in range(HALVES)
        ]
        a = each(lambda l, v: l * v, lam, near)
        near_lag = each(lambda l, v, c: l * v + c, lam, near_lag, a)
        near = [[a[g][h] + each_sum[h] for h in range(HALVES)] for g in range(GROUPS)]
    first = each(lambda f, n: f + n, first, near)
    second = each(lambda f, n: f + n, second, near_lag)
    last = [gains, [jnp.zeros((SUB, LANES), f32)] * HALVES]
    sent = [state, plain, moment, tiles(p_ref), tiles(w_ref), first, second, last]
    flat_ref = send_ref.reshape(CHUNKS * SUB, LANES)
    for q in range(SUB):
        for g in range(GROUPS):
            for h in range(HALVES):
                at = g * SUB * HALVES * SUB + h * SUB + q
                flat_ref[pl.ds(at, SUB, stride=HALVES * SUB), :] = sent[q][g][h]
    for store in stores:
        store.wait()


def shifted(value, k):
    index = lax.broadcasted_iota(jnp.int32, (CHUNKS, LANES), 0)
    return jnp.where(index >= k, pltpu.roll(value, k, 0), 0.0)


def shifted_back(value, k):
    index = lax.broadcasted_iota(jnp.int32, (CHUNKS, LANES), 0)
    return jnp.where(index < CHUNKS - k, pltpu.roll(value, CHUNKS - k, 0), 0.0)


def owner_kernel(recv_ref, log_rate_ref, residue_ref, send_ref):
    flat_ref = recv_ref.reshape(CHUNKS * SUB, LANES)
    state, plain, moment, p, w, first, second, gains = (
        flat_ref[pl.ds(q, CHUNKS, stride=SUB), :] for q in range(SUB)
    )
    rate = jnp.exp(log_rate_ref[...])
    res = residue_ref[...]
    lam = jnp.exp(-rate)
    whole, whole_u, whole_q, back = state, plain, moment, p
    for step in (1, 2, 4, 8, 16):
        far = jnp.exp(rate * (-float(ROWS * step)))
        before = shifted(whole, step)
        whole_q = whole_q + far * (shifted(whole_q, step) + float(ROWS * step) * before)
        whole = whole + far * before
        whole_u = whole_u + far * shifted(whole_u, step)
        back = back + far * shifted_back(back, step)
    into, into_u, into_q = shifted(whole, 1), shifted(whole_u, 1), shifted(whole_q, 1)
    into_p = shifted_back(back, 1)
    scale = 1.0 / math.sqrt(ROWS * CHUNKS)
    grad_residue = jnp.sum(first + lam * (into * p), axis=0, keepdims=True)
    weighted = jnp.sum(second + lam * ((w + p) * into + p * into_q), axis=0, keepdims=True)
    grad_gain = jnp.sum(gains + res * (lam * (into_u * p)), axis=0, keepdims=True)
    shape = (CHUNKS, LANES)
    rows = [
        into,
        into_p,
        jnp.broadcast_to(grad_residue * scale, shape),
        jnp.broadcast_to(-rate * res * weighted * scale, shape),
        jnp.broadcast_to(grad_gain * scale, shape),
    ]
    rows += [jnp.zeros(shape, f32)] * (SUB - len(rows))
    flat_ref = send_ref.reshape(CHUNKS * SUB, LANES)
    for q in range(SUB):
        flat_ref[pl.ds(q, CHUNKS, stride=SUB), :] = rows[q]


def received(ref, q):
    stride = HALVES * SUB
    flat_ref = ref.reshape(CHUNKS * SUB, LANES)
    return [
        [
            flat_ref[pl.ds(g * SUB * stride + h * SUB + q, SUB, stride=stride), :]
            for h in range(HALVES)
        ]
        for g in range(GROUPS)
    ]


def fill_totals(
    recv_ref,
    local_ref,
    log_rate_ref,
    residue_ref,
    total_ref,
    into_ref,
    fade_ref,
    rate_ref,
    weight_ref,
):
    fill_fade(log_rate_ref, residue_ref, fade_ref, rate_ref, weight_ref)
    into = received(recv_ref, 1)
    step = each(lambda v: jnp.exp(jnp.exp(v) * (-float(SPAN))), tiles(log_rate_ref))
    spans = ROWS // SPAN
    for b in reversed(range(spans)):
        for g in range(GROUPS):
            for h in range(HALVES):
                into_ref[tile_rows(b * MODES * HALVES, g, h), :] = into[g][h]
        into = each(lambda l, v: l * v, step, into)
    places = [
        [(g * HALVES + h) * SUB + m for g in range(GROUPS) for m in range(SUB)]
        for h in range(HALVES)
    ]

    def block(b, carry):
        for h in range(HALVES):
            rows = [into_ref[pl.ds(b * MODES * HALVES + at, SUB, stride=0), :] for at in places[h]]
            for k in range(SPAN // SUB):
                own = span(pl.multiple_of(b * SPAN + k * SUB, SUB), SUB, h)
                terms = [
                    fade_ref[pl.ds(at * SPAN + k * SUB, SUB), :] * rows[m]
                    for m, at in enumerate(places[h])
                ]
                while len(terms) > 1:
                    terms = [a + b for a, b in zip(terms[::2], terms[1::2])]
                total_ref[own] = local_ref[own] + terms[0]
        return carry

    lax.fori_loop(0, spans, block, 0)


def correct_kernel(
    recv_ref,
    local_ref,
    full_ref,
    log_rate_ref,
    residue_ref,
    send_ref,
    total_ref,
    into_ref,
    fade_ref,
    rate_ref,
    weight_ref,
):
    fill_totals(
        recv_ref,
        local_ref,
        log_rate_ref,
        residue_ref,
        total_ref,
        into_ref,
        fade_ref,
        rate_ref,
        weight_ref,
    )
    parts = []
    for k in range(QUARTERS):
        own = [span(k * LANES, LANES, h) for h in range(HALVES)]
        parts.append(lane_totals(sum(total_ref[at] * full_ref[at] for at in own)))
    send_rows(send_ref, parts)


def forward_kernel(
    recv_ref,
    signal_ref,
    inv_ref,
    local_ref,
    stream_ref,
    key_ref,
    query_ref,
    grad_ref,
    gain_ref,
    log_rate_ref,
    residue_ref,
    output_ref,
    grad_key_ref,
    grad_query_ref,
    left_ref,
    right_ref,
    grad_residue_ref,
    grad_rate_ref,
    grad_gain_ref,
    conv_ref,
    x_ref,
    total_ref,
    into_ref,
    fade_ref,
    rate_ref,
    weight_ref,
):
    fill_totals(
        recv_ref,
        local_ref,
        log_rate_ref,
        residue_ref,
        total_ref,
        into_ref,
        fade_ref,
        rate_ref,
        weight_ref,
    )
    x_ref[...] = signal_ref[...].astype(f32)
    lam = each(lambda v: jnp.exp(-jnp.exp(v)), tiles(log_rate_ref))
    res = tiles(residue_ref)

    def block(i, state):
        base = pl.multiple_of(i * SUB, SUB)
        parts = [[None] * SUB for _ in range(HALVES)]
        for k in range(SUB):
            xs = [row(x_ref, base + k, h) for h in range(HALVES)]
            state = [
                [lam[g][h] * state[g][h] + xs[h] for h in range(HALVES)] for g in range(GROUPS)
            ]
            for h in range(HALVES):
                parts[h][k] = res[0][h] * state[0][h] + res[1][h] * state[1][h]
        for h in range(HALVES):
            conv_ref[span(base, SUB, h)] = fold_sublanes(parts[h])
        return state

    lax.fori_loop(0, BLOCKS, block, received(recv_ref, 0))
    gain = gain_ref[...]
    for k in range(4):
        part = pl.ds(k * LANES, LANES)
        inv = inv_ref[part, :]
        for h in range(HALVES):
            at = (part, lane(h))
            own = span(k * LANES, LANES, h)
            conv = conv_ref[own]
            output_ref[at] = (query_ref[at].astype(f32) * conv).astype(bf16)
            grad_query_ref[at] = (grad_ref[at].astype(f32) * conv).astype(bf16)
            unit = stream_ref[at].astype(f32) * inv
            total = total_ref[own]
            own_gain = gain[:, lane_slice(h)]
            grad_key_ref[at] = (total * (unit * own_gain)).astype(bf16)
            left_ref[own] = inv * (total * key_ref[at].astype(f32) * own_gain)
            right_ref[own] = inv * unit
    for q, ref in ((2, grad_residue_ref), (3, grad_rate_ref)):
        found = received(recv_ref, q)
        for g in range(GROUPS):
            for h in range(HALVES):
                ref[g * SUB : (g + 1) * SUB, lane(h)] = found[g][h]
    found = received(recv_ref, 4)
    for h in range(HALVES):
        grad_gain_ref[:, lane(h)] = jnp.sum(found[0][h] + found[1][h], axis=0, keepdims=True)


def finish_kernel(recv_ref, left_ref, right_ref, grad_stream_ref):
    inner = columns(jnp.sum(recv_ref[...], axis=0) / D)
    for k in range(QUARTERS):
        part = pl.ds(k * LANES, LANES)
        across = jnp.broadcast_to(inner[k], (LANES, LANES))
        for h in range(HALVES):
            own = span(k * LANES, LANES, h)
            value = left_ref[own] - right_ref[own] * across
            grad_stream_ref[part, lane(h)] = value.astype(bf16)


def in_hbm(value):
    return pltpu.with_memory_space_constraint(value, pltpu.HBM)


def exchange(value, axis):
    return lax.all_to_all(value, axis, split_axis=0, concat_axis=0, tiled=True)


def local(stream, key_gate, query_gate, grad_output, norm_gain, residue, log_rate):
    wide = (ROWS, COLS)
    split = (HALVES * ROWS, LANES)
    modes = (MODES, COLS)
    tile = (CH, SUB, LANES)
    (squares,) = call(square_kernel, "v", [(tile, f32, "v")], name="square")(stream)
    squares = exchange(squares, "ch")
    log_rate_t = log_rate.T
    residue_t = residue.T
    me = lax.axis_index("ctx")
    log_rate_own = lax.dynamic_slice_in_dim(log_rate_t.reshape(CHUNKS, LANES), me, 1, 0)
    residue_own = lax.dynamic_slice_in_dim(residue_t.reshape(CHUNKS, LANES), me, 1, 0)
    table = (BLOCKS * MODES * HALVES, LANES)
    packed = (CHUNKS, SUB, LANES)
    own = (1, LANES)
    (
        grad_conv,
        local_grad,
        p,
        w,
        across,
        across_lag,
        gain,
        log_rate_own,
        residue_own,
    ) = call(
        adjoint_kernel,
        "v" * 7,
        [
            ((HALVES * BLOCKS, SUB, LANES), f32, "a"),
            (split, f32, "a"),
            (modes, f32, "v"),
            (modes, f32, "v"),
            (table, f32, "v"),
            (table, f32, "v"),
            ((1, COLS), f32, "v"),
            (own, f32, "v"),
            (own, f32, "v"),
        ],
        [pltpu.VMEM(split, f32), pltpu.VMEM(split, f32), pltpu.SemaphoreType.DMA((2,))],
        name="adjoint",
    )(
        query_gate,
        grad_output,
        log_rate_t,
        residue_t,
        norm_gain[None, :],
        log_rate_own,
        residue_own,
    )
    rows = (ROWS, LANES)
    sent, signal, inv, full = call(
        state_kernel,
        "vvvvaavvvvv",
        [(packed, f32, "v"), (split, bf16, "a"), (rows, f32, "a"), (split, f32, "v")],
        [
            pltpu.VMEM(split, bf16),
            pltpu.VMEM(rows, f32),
            pltpu.VMEM(split, f32),
            pltpu.VMEM(split, f32),
            pltpu.VMEM(split, f32),
            pltpu.VMEM((2 * HALVES * ROWS, LANES), f32),
            pltpu.SemaphoreType.DMA((4,)),
        ],
        name="state",
    )(
        squares,
        stream,
        key_gate,
        gain,
        in_hbm(grad_conv),
        in_hbm(local_grad),
        p,
        w,
        across,
        across_lag,
        log_rate_t,
    )
    got = exchange(sent, "ctx")
    (sent,) = call(owner_kernel, "vvv", [(packed, f32, "v")], name="owner")(
        got, log_rate_own, residue_own
    )
    got = exchange(sent, "ctx")
    totals = [
        pltpu.VMEM(split, f32),
        pltpu.VMEM((ROWS // SPAN * MODES * HALVES, LANES), f32),
        pltpu.VMEM((MODES * HALVES * SPAN, LANES), f32),
        pltpu.VMEM((MODES * HALVES, LANES), f32),
        pltpu.VMEM((MODES * HALVES, LANES), f32),
    ]
    (inner,) = call(correct_kernel, "vvvvv", [(tile, f32, "v")], totals, name="correct")(
        got, local_grad, full, log_rate_t, residue_t
    )
    inner = exchange(inner, "ch")
    output, grad_key, grad_query, left, right, grad_residue, grad_rate, grad_gain = call(
        forward_kernel,
        "v" * 11,
        [
            (wide, bf16, "v"),
            (wide, bf16, "v"),
            (wide, bf16, "v"),
            (split, f32, "v"),
            (split, f32, "v"),
            (modes, f32, "v"),
            (modes, f32, "v"),
            ((1, COLS), f32, "v"),
        ],
        [pltpu.VMEM(split, f32), pltpu.VMEM(split, f32), *totals],
        name="forward",
    )(
        got,
        signal,
        inv,
        local_grad,
        stream,
        key_gate,
        query_gate,
        grad_output,
        gain,
        log_rate_t,
        residue_t,
    )
    (grad_stream,) = call(finish_kernel, "vvv", [(wide, bf16, "v")], name="finish")(
        inner, left, right
    )
    return (
        output,
        grad_stream,
        grad_key,
        grad_query,
        grad_gain[0],
        grad_residue.T,
        grad_rate.T,
    )


def solution(mesh):
    placed = (
        P("ctx", "ch"),
        P("ctx", "ch"),
        P("ctx", "ch"),
        P("ctx", "ch"),
        P("ch"),
        P("ch", None),
        P("ch", None),
    )
    return jax.shard_map(
        local,
        mesh=mesh,
        in_specs=placed,
        out_specs=(
            P("ctx", "ch"),
            P("ctx", "ch"),
            P("ctx", "ch"),
            P("ctx", "ch"),
            P("ch"),
            P("ch", None),
            P("ch", None),
        ),
        check_vma=False,
    )
```

```python
import math

import jax
import jax.numpy as jnp
from jax import lax
from jax.experimental import pallas as pl
from jax.experimental.pallas import tpu as pltpu
from jax.sharding import PartitionSpec as P

D = 4096
MODES = 16
ROWS = 512
COLS = 256
CHUNKS = 32
CH = 16
LANES = 128
SUB = 8
BLOCKS = ROWS // SUB
SPAN = 16
QUARTERS = ROWS // LANES
HALVES = COLS // LANES
GROUPS = MODES // SUB
epsilon = 1e-05
f32 = jnp.float32
bf16 = jnp.bfloat16


def call(kernel, ins, outs, scratch=(), limit=8, flops=1 << 22, name=None):
    held = {"v": pl.BlockSpec(memory_space=pltpu.VMEM), "a": pl.BlockSpec(memory_space=pltpu.HBM)}
    return pl.pallas_call(
        kernel,
        in_specs=[held[k] for k in ins],
        out_specs=tuple(held[k] for _, _, k in outs),
        out_shape=tuple(
            pltpu.HBM(s, d) if k == "a" else jax.ShapeDtypeStruct(s, d) for s, d, k in outs
        ),
        scratch_shapes=list(scratch),
        compiler_params=pltpu.CompilerParams(vmem_limit_bytes=limit << 20),
        cost_estimate=pl.CostEstimate(flops=flops, bytes_accessed=1 << 21, transcendentals=0),
        name=name,
    )


def lane(half):
    return pl.ds(half * LANES, LANES)


def lane_slice(half):
    return slice(half * LANES, (half + 1) * LANES)


def tiles(ref):
    return [[ref[g * SUB : (g + 1) * SUB, lane(h)] for h in range(HALVES)] for g in range(GROUPS)]


def each(fn, *args):
    return [[fn(*(a[g][h] for a in args)) for h in range(HALVES)] for g in range(GROUPS)]


def zeros_tiles():
    return [[jnp.zeros((SUB, LANES), f32) for _ in range(HALVES)] for _ in range(GROUPS)]


def fold_sublanes(parts):
    sub = lax.broadcasted_iota(jnp.int32, (SUB, LANES), 0)
    low4 = sub < 4
    low2 = (sub & 2) == 0
    low1 = (sub & 1) == 0
    four = []
    for k in range(4):
        a, b = parts[k], parts[k + 4]
        four.append(jnp.where(low4, a, b) + pltpu.roll(jnp.where(low4, b, a), 4, 0))
    two = []
    for k in range(2):
        a, b = four[k], four[k + 2]
        two.append(jnp.where(low2, a + pltpu.roll(a, 6, 0), b + pltpu.roll(b, 2, 0)))
    a, b = two
    return jnp.where(low1, a + pltpu.roll(a, 7, 0), b + pltpu.roll(b, 1, 0))


def row(ref, t, half):
    return ref[pl.ds(half * ROWS + t, SUB, stride=0), :]


def span(start, size, half):
    return (pl.ds(half * ROWS + start, size), slice(None))


def lane_totals(values):
    return jnp.broadcast_to(jnp.sum(values.T, axis=0, keepdims=True), (SUB, LANES))


def send_rows(ref, parts):
    sub = lax.broadcasted_iota(jnp.int32, (SUB, LANES), 0) & 3
    tile = parts[0]
    for k in range(1, QUARTERS):
        tile = jnp.where(sub == k, parts[k], tile)
    ref[...] = jnp.broadcast_to(tile[None], (CH, SUB, LANES))


def columns(tile):
    turned = tile.T
    return [turned[:, k : k + 1] for k in range(4)]


def square_kernel(stream_ref, send_ref):
    parts = []
    for k in range(QUARTERS):
        part = pl.ds(k * LANES, LANES)
        wide = [stream_ref[part, lane(h)].astype(f32) for h in range(HALVES)]
        parts.append(lane_totals(sum(v * v for v in wide)))
    send_rows(send_ref, parts)


def tile_rows(start, group, half):
    return pl.ds(start + (group * HALVES + half) * SUB, SUB)


def adjoint_kernel(
    query_ref,
    grad_ref,
    log_rate_ref,
    residue_ref,
    gain_ref,
    own_log_rate_ref,
    own_residue_ref,
    g_out,
    local_out,
    p_ref,
    w_ref,
    across_ref,
    across_lag_ref,
    gain_out,
    own_log_rate_out,
    own_residue_out,
    g_ref,
    local_ref,
    done,
):
    gain_out[...] = gain_ref[...]
    own_log_rate_out[...] = own_log_rate_ref[...]
    own_residue_out[...] = own_residue_ref[...]
    for h in range(HALVES):
        g_ref[span(0, ROWS, h)] = grad_ref[:, lane(h)].astype(f32) * query_ref[
            :, lane(h)
        ].astype(f32)
    g_copy = pltpu.make_async_copy(
        g_ref.reshape(HALVES * BLOCKS, SUB, LANES), g_out, done.at[1]
    )
    g_copy.start()
    rate = each(jnp.exp, tiles(log_rate_ref))
    lam = each(lambda v: jnp.exp(-v), rate)
    lam_block = each(lambda v: jnp.exp(v * (-float(SUB))), rate)
    res = tiles(residue_ref)

    def block(i, carry):
        p, w = carry
        index = BLOCKS - 1 - i
        base = pl.multiple_of(index * SUB, SUB)
        parts = [[None] * SUB for _ in range(HALVES)]
        near, near_w = None, None
        far, far_w = p, w
        for k in reversed(range(SUB)):
            rows = [row(g_ref, base + k, h) for h in range(HALVES)]
            p = [[lam[g][h] * p[g][h] + rows[h] for h in range(HALVES)] for g in range(GROUPS)]
            for h in range(HALVES):
                parts[h][k] = res[0][h] * p[0][h] + res[1][h] * p[1][h]
            if near is None:
                near = [rows, rows]
            else:
                a = each(lambda l, v: l * v, lam, near)
                if near_w is None:
                    near_w = a
                else:
                    near_w = each(lambda l, v, c: l * v + c, lam, near_w, a)
                near = [[a[g][h] + rows[h] for h in range(HALVES)] for g in range(GROUPS)]
        w = each(
            lambda n, l, v, q: n + l * (v + float(SUB) * q), near_w, lam_block, far_w, far
        )
        start = pl.multiple_of(index * (MODES * HALVES), SUB)
        for g in range(GROUPS):
            for h in range(HALVES):
                at = tile_rows(start, g, h)
                across_ref[at, :] = lam[g][h] * near[g][h]
                across_lag_ref[at, :] = lam[g][h] * (near_w[g][h] + near[g][h])
        for h in range(HALVES):
            local_ref[span(base, SUB, h)] = fold_sublanes(parts[h])
        return p, w

    p, w = lax.fori_loop(0, BLOCKS, block, (zeros_tiles(), zeros_tiles()))
    copy = pltpu.make_async_copy(local_ref, local_out, done.at[0])
    copy.start()
    for g in range(GROUPS):
        for h in range(HALVES):
            p_ref[g * SUB : (g + 1) * SUB, lane(h)] = p[g][h]
            w_ref[g * SUB : (g + 1) * SUB, lane(h)] = w[g][h]
    copy.wait()
    g_copy.wait()


def fill_fade(log_rate_ref, residue_ref, fade_ref, rate_ref, weight_ref):
    sub = lax.broadcasted_iota(jnp.int32, (SUB, LANES), 0)
    rate = each(jnp.exp, tiles(log_rate_ref))
    res = tiles(residue_ref)
    for g in range(GROUPS):
        for h in range(HALVES):
            rate_ref[tile_rows(0, g, h), :] = rate[g][h]
            weight_ref[tile_rows(0, g, h), :] = res[g][h]

    def block(at, carry):
        own_rate = rate_ref[pl.ds(at, SUB, stride=0), :]
        own_weight = weight_ref[pl.ds(at, SUB, stride=0), :]
        for k in range(SPAN // SUB):
            power = (sub + (k * SUB - SPAN)).astype(f32)
            rows = pl.ds(pl.multiple_of(at * SPAN + k * SUB, SUB), SUB)
            fade_ref[rows, :] = own_weight * jnp.exp(own_rate * power)
        return carry

    lax.fori_loop(0, MODES * HALVES, block, 0, unroll=8)


def state_kernel(
    recv_ref,
    stream_ref,
    key_ref,
    gain_ref,
    g_in,
    local_in,
    p_ref,
    w_ref,
    across_ref,
    across_lag_ref,
    log_rate_ref,
    send_ref,
    signal_out,
    inv_out,
    full_ref,
    signal_ref,
    inv_ref,
    local_ref,
    x_ref,
    u_ref,
    padded_ref,
    done,
):
    fetch = pltpu.make_async_copy(local_in, local_ref, done.at[0])
    fetch.start()
    wider_ref = padded_ref.reshape(HALVES * BLOCKS, 2 * SUB, LANES)
    fetch_g = pltpu.make_async_copy(g_in, wider_ref.at[:, pl.ds(0, SUB), :], done.at[3])
    fetch_g.start()
    total = jnp.sum(recv_ref[...], axis=0)
    inverse = columns(lax.rsqrt(total / D + epsilon))
    gain = gain_ref[...]
    for k in range(4):
        part = pl.ds(k * LANES, LANES)
        inv = jnp.broadcast_to(inverse[k], (LANES, LANES))
        inv_ref[part, :] = inv
        for h in range(HALVES):
            unit = stream_ref[part, lane(h)].astype(f32) * inv
            key = key_ref[part, lane(h)].astype(f32)
            own = span(k * LANES, LANES, h)
            u_ref[own] = key * unit
            signal = key * (unit * gain[:, lane_slice(h)])
            full_ref[own] = signal
            narrow = signal.astype(bf16)
            signal_ref[own] = narrow
            x_ref[own] = narrow.astype(f32)
    stores = [
        pltpu.make_async_copy(signal_ref, signal_out, done.at[1]),
        pltpu.make_async_copy(inv_ref, inv_out, done.at[2]),
    ]
    for copy in stores:
        copy.start()
    lam = each(lambda v: jnp.exp(-jnp.exp(v)), tiles(log_rate_ref))

    def block(i, carry):
        state, moment, plain, first, second = carry
        base = pl.multiple_of(i * SUB, SUB)
        start = pl.multiple_of(i * (MODES * HALVES), SUB)
        near = [[across_ref[tile_rows(start, g, h), :] for h in range(HALVES)] for g in range(GROUPS)]
        near_lag = [
            [across_lag_ref[tile_rows(start, g, h), :] for h in range(HALVES)]
            for g in range(GROUPS)
        ]
        first = each(lambda f, s, n: f + s * n, first, state, near)
        second = each(
            lambda f, s, n, m, v: f + (s * n + m * v), second, state, near_lag, moment, near
        )
        for h in range(HALVES):
            wider = pl.multiple_of((h * BLOCKS + i) * 2 * SUB, 2 * SUB)
            padded_ref[pl.ds(wider + SUB, SUB), :] = jnp.zeros((SUB, LANES), f32)
        for k in range(SUB):
            xs = [row(x_ref, base + k, h) for h in range(HALVES)]
            us = [row(u_ref, base + k, h) for h in range(HALVES)]
            a = each(lambda l, v: l * v, lam, state)
            moment = each(lambda l, v, c: l * v + c, lam, moment, a)
            state = [[a[g][h] + xs[h] for h in range(HALVES)] for g in range(GROUPS)]
            plain = [
                [lam[g][h] * plain[g][h] + us[h] for h in range(HALVES)] for g in range(GROUPS)
            ]
        return state, moment, plain, first, second

    zero = zeros_tiles
    start = (zero(), zero(), zero(), zero(), zero())
    state, moment, plain, first, second = lax.fori_loop(0, BLOCKS, block, start, unroll=4)


    def inside(i, carry):
        sums, gains = carry
        base = pl.multiple_of(i * SUB, SUB)
        new_sums, new_gains = [], []
        for h in range(HALVES):
            at = span(base, SUB, h)
            x = x_ref[at]
            new_gains.append(gains[h] + u_ref[at] * local_ref[at])
            wider = pl.multiple_of((h * BLOCKS + i) * 2 * SUB, 2 * SUB)
            own = [
                sums[h][d] + x * padded_ref[pl.ds(wider + d, SUB), :] for d in range(SUB)
            ]
            new_sums.append(own)
        return new_sums, new_gains

    fetch.wait()
    fetch_g.wait()
    none = jnp.zeros((SUB, LANES), f32)
    sums, gains = lax.fori_loop(
        0, BLOCKS, inside, ([[none] * SUB for _ in range(HALVES)], [none] * HALVES), unroll=8
    )
    near, near_lag = zero(), zero()
    for d in reversed(range(SUB)):
        each_sum = [
            jnp.broadcast_to(jnp.sum(sums[h][d], axis=0, keepdims=True), (SUB, LANES))
            for h in range(HALVES)
        ]
        a = each(lambda l, v: l * v, lam, near)
        near_lag = each(lambda l, v, c: l * v + c, lam, near_lag, a)
        near = [[a[g][h] + each_sum[h] for h in range(HALVES)] for g in range(GROUPS)]
    first = each(lambda f, n: f + n, first, near)
    second = each(lambda f, n: f + n, second, near_lag)
    last = [gains, [jnp.zeros((SUB, LANES), f32)] * HALVES]
    sent = [state, plain, moment, tiles(p_ref), tiles(w_ref), first, second, last]
    flat_ref = send_ref.reshape(CHUNKS * SUB, LANES)
    for q in range(SUB):
        for g in range(GROUPS):
            for h in range(HALVES):
                at = g * SUB * HALVES * SUB + h * SUB + q
                flat_ref[pl.ds(at, SUB, stride=HALVES * SUB), :] = sent[q][g][h]
    for store in stores:
        store.wait()


def shifted(value, k):
    index = lax.broadcasted_iota(jnp.int32, (CHUNKS, LANES), 0)
    return jnp.where(index >= k, pltpu.roll(value, k, 0), 0.0)


def shifted_back(value, k):
    index = lax.broadcasted_iota(jnp.int32, (CHUNKS, LANES), 0)
    return jnp.where(index < CHUNKS - k, pltpu.roll(value, CHUNKS - k, 0), 0.0)


def owner_kernel(recv_ref, log_rate_ref, residue_ref, send_ref):
    flat_ref = recv_ref.reshape(CHUNKS * SUB, LANES)
    state, plain, moment, p, w, first, second, gains = (
        flat_ref[pl.ds(q, CHUNKS, stride=SUB), :] for q in range(SUB)
    )
    rate = jnp.exp(log_rate_ref[...])
    res = residue_ref[...]
    lam = jnp.exp(-rate)
    whole, whole_u, whole_q, back = state, plain, moment, p
    for step in (1, 2, 4, 8, 16):
        far = jnp.exp(rate * (-float(ROWS * step)))
        before = shifted(whole, step)
        whole_q = whole_q + far * (shifted(whole_q, step) + float(ROWS * step) * before)
        whole = whole + far * before
        whole_u = whole_u + far * shifted(whole_u, step)
        back = back + far * shifted_back(back, step)
    into, into_u, into_q = shifted(whole, 1), shifted(whole_u, 1), shifted(whole_q, 1)
    into_p = shifted_back(back, 1)
    scale = 1.0 / math.sqrt(ROWS * CHUNKS)
    grad_residue = jnp.sum(first + lam * (into * p), axis=0, keepdims=True)
    weighted = jnp.sum(second + lam * ((w + p) * into + p * into_q), axis=0, keepdims=True)
    grad_gain = jnp.sum(gains + res * (lam * (into_u * p)), axis=0, keepdims=True)
    shape = (CHUNKS, LANES)
    rows = [
        into,
        into_p,
        jnp.broadcast_to(grad_residue * scale, shape),
        jnp.broadcast_to(-rate * res * weighted * scale, shape),
        jnp.broadcast_to(grad_gain * scale, shape),
    ]
    rows += [jnp.zeros(shape, f32)] * (SUB - len(rows))
    flat_ref = send_ref.reshape(CHUNKS * SUB, LANES)
    for q in range(SUB):
        flat_ref[pl.ds(q, CHUNKS, stride=SUB), :] = rows[q]


def received(ref, q):
    stride = HALVES * SUB
    flat_ref = ref.reshape(CHUNKS * SUB, LANES)
    return [
        [
            flat_ref[pl.ds(g * SUB * stride + h * SUB + q, SUB, stride=stride), :]
            for h in range(HALVES)
        ]
        for g in range(GROUPS)
    ]


def fill_totals(
    recv_ref,
    local_ref,
    log_rate_ref,
    residue_ref,
    total_ref,
    into_ref,
    fade_ref,
    rate_ref,
    weight_ref,
):
    fill_fade(log_rate_ref, residue_ref, fade_ref, rate_ref, weight_ref)
    into = received(recv_ref, 1)
    step = each(lambda v: jnp.exp(jnp.exp(v) * (-float(SPAN))), tiles(log_rate_ref))
    spans = ROWS // SPAN
    for b in reversed(range(spans)):
        for g in range(GROUPS):
            for h in range(HALVES):
                into_ref[tile_rows(b * MODES * HALVES, g, h), :] = into[g][h]
        into = each(lambda l, v: l * v, step, into)
    places = [
        [(g * HALVES + h) * SUB + m for g in range(GROUPS) for m in range(SUB)]
        for h in range(HALVES)
    ]

    def block(b, carry):
        for h in range(HALVES):
            rows = [into_ref[pl.ds(b * MODES * HALVES + at, SUB, stride=0), :] for at in places[h]]
            for k in range(SPAN // SUB):
                own = span(pl.multiple_of(b * SPAN + k * SUB, SUB), SUB, h)
                terms = [
                    fade_ref[pl.ds(at * SPAN + k * SUB, SUB), :] * rows[m]
                    for m, at in enumerate(places[h])
                ]
                while len(terms) > 1:
                    terms = [a + b for a, b in zip(terms[::2], terms[1::2])]
                total_ref[own] = local_ref[own] + terms[0]
        return carry

    lax.fori_loop(0, spans, block, 0, unroll=4)


def correct_kernel(
    recv_ref,
    local_ref,
    full_ref,
    log_rate_ref,
    residue_ref,
    send_ref,
    total_ref,
    into_ref,
    fade_ref,
    rate_ref,
    weight_ref,
):
    fill_totals(
        recv_ref,
        local_ref,
        log_rate_ref,
        residue_ref,
        total_ref,
        into_ref,
        fade_ref,
        rate_ref,
        weight_ref,
    )
    parts = []
    for k in range(QUARTERS):
        own = [span(k * LANES, LANES, h) for h in range(HALVES)]
        parts.append(lane_totals(sum(total_ref[at] * full_ref[at] for at in own)))
    send_rows(send_ref, parts)


def forward_kernel(
    recv_ref,
    signal_ref,
    inv_ref,
    local_ref,
    stream_ref,
    key_ref,
    query_ref,
    grad_ref,
    gain_ref,
    log_rate_ref,
    residue_ref,
    output_ref,
    grad_key_ref,
    grad_query_ref,
    left_ref,
    right_ref,
    grad_residue_ref,
    grad_rate_ref,
    grad_gain_ref,
    conv_ref,
    x_ref,
    total_ref,
    into_ref,
    fade_ref,
    rate_ref,
    weight_ref,
):
    fill_totals(
        recv_ref,
        local_ref,
        log_rate_ref,
        residue_ref,
        total_ref,
        into_ref,
        fade_ref,
        rate_ref,
        weight_ref,
    )
    x_ref[...] = signal_ref[...].astype(f32)
    lam = each(lambda v: jnp.exp(-jnp.exp(v)), tiles(log_rate_ref))
    res = tiles(residue_ref)

    def block(i, state):
        base = pl.multiple_of(i * SUB, SUB)
        parts = [[None] * SUB for _ in range(HALVES)]
        for k in range(SUB):
            xs = [row(x_ref, base + k, h) for h in range(HALVES)]
            state = [
                [lam[g][h] * state[g][h] + xs[h] for h in range(HALVES)] for g in range(GROUPS)
            ]
            for h in range(HALVES):
                parts[h][k] = res[0][h] * state[0][h] + res[1][h] * state[1][h]
        for h in range(HALVES):
            conv_ref[span(base, SUB, h)] = fold_sublanes(parts[h])
        return state

    lax.fori_loop(0, BLOCKS, block, received(recv_ref, 0))
    gain = gain_ref[...]
    for k in range(4):
        part = pl.ds(k * LANES, LANES)
        inv = inv_ref[part, :]
        for h in range(HALVES):
            at = (part, lane(h))
            own = span(k * LANES, LANES, h)
            conv = conv_ref[own]
            output_ref[at] = (query_ref[at].astype(f32) * conv).astype(bf16)
            grad_query_ref[at] = (grad_ref[at].astype(f32) * conv).astype(bf16)
            unit = stream_ref[at].astype(f32) * inv
            total = total_ref[own]
            own_gain = gain[:, lane_slice(h)]
            grad_key_ref[at] = (total * (unit * own_gain)).astype(bf16)
            left_ref[own] = inv * (total * key_ref[at].astype(f32) * own_gain)
            right_ref[own] = inv * unit
    for q, ref in ((2, grad_residue_ref), (3, grad_rate_ref)):
        found = received(recv_ref, q)
        for g in range(GROUPS):
            for h in range(HALVES):
                ref[g * SUB : (g + 1) * SUB, lane(h)] = found[g][h]
    found = received(recv_ref, 4)
    for h in range(HALVES):
        grad_gain_ref[:, lane(h)] = jnp.sum(found[0][h] + found[1][h], axis=0, keepdims=True)


def finish_kernel(recv_ref, left_ref, right_ref, grad_stream_ref):
    inner = columns(jnp.sum(recv_ref[...], axis=0) / D)
    for k in range(QUARTERS):
        part = pl.ds(k * LANES, LANES)
        across = jnp.broadcast_to(inner[k], (LANES, LANES))
        for h in range(HALVES):
            own = span(k * LANES, LANES, h)
            value = left_ref[own] - right_ref[own] * across
            grad_stream_ref[part, lane(h)] = value.astype(bf16)


def in_hbm(value):
    return pltpu.with_memory_space_constraint(value, pltpu.HBM)


def exchange(value, axis):
    return lax.all_to_all(value, axis, split_axis=0, concat_axis=0, tiled=True)


def local(stream, key_gate, query_gate, grad_output, norm_gain, residue, log_rate):
    wide = (ROWS, COLS)
    split = (HALVES * ROWS, LANES)
    modes = (MODES, COLS)
    tile = (CH, SUB, LANES)
    (squares,) = call(square_kernel, "v", [(tile, f32, "v")], name="square")(stream)
    squares = exchange(squares, "ch")
    log_rate_t = log_rate.T
    residue_t = residue.T
    me = lax.axis_index("ctx")
    log_rate_own = lax.dynamic_slice_in_dim(log_rate_t.reshape(CHUNKS, LANES), me, 1, 0)
    residue_own = lax.dynamic_slice_in_dim(residue_t.reshape(CHUNKS, LANES), me, 1, 0)
    table = (BLOCKS * MODES * HALVES, LANES)
    packed = (CHUNKS, SUB, LANES)
    own = (1, LANES)
    (
        grad_conv,
        local_grad,
        p,
        w,
        across,
        across_lag,
        gain,
        log_rate_own,
        residue_own,
    ) = call(
        adjoint_kernel,
        "v" * 7,
        [
            ((HALVES * BLOCKS, SUB, LANES), f32, "a"),
            (split, f32, "a"),
            (modes, f32, "v"),
            (modes, f32, "v"),
            (table, f32, "v"),
            (table, f32, "v"),
            ((1, COLS), f32, "v"),
            (own, f32, "v"),
            (own, f32, "v"),
        ],
        [pltpu.VMEM(split, f32), pltpu.VMEM(split, f32), pltpu.SemaphoreType.DMA((2,))],
        name="adjoint",
    )(
        query_gate,
        grad_output,
        log_rate_t,
        residue_t,
        norm_gain[None, :],
        log_rate_own,
        residue_own,
    )
    rows = (ROWS, LANES)
    sent, signal, inv, full = call(
        state_kernel,
        "vvvvaavvvvv",
        [(packed, f32, "v"), (split, bf16, "a"), (rows, f32, "a"), (split, f32, "v")],
        [
            pltpu.VMEM(split, bf16),
            pltpu.VMEM(rows, f32),
            pltpu.VMEM(split, f32),
            pltpu.VMEM(split, f32),
            pltpu.VMEM(split, f32),
            pltpu.VMEM((2 * HALVES * ROWS, LANES), f32),
            pltpu.SemaphoreType.DMA((4,)),
        ],
        name="state",
    )(
        squares,
        stream,
        key_gate,
        gain,
        in_hbm(grad_conv),
        in_hbm(local_grad),
        p,
        w,
        across,
        across_lag,
        log_rate_t,
    )
    got = exchange(sent, "ctx")
    (sent,) = call(owner_kernel, "vvv", [(packed, f32, "v")], name="owner")(
        got, log_rate_own, residue_own
    )
    got = exchange(sent, "ctx")
    totals = [
        pltpu.VMEM(split, f32),
        pltpu.VMEM((ROWS // SPAN * MODES * HALVES, LANES), f32),
        pltpu.VMEM((MODES * HALVES * SPAN, LANES), f32),
        pltpu.VMEM((MODES * HALVES, LANES), f32),
        pltpu.VMEM((MODES * HALVES, LANES), f32),
    ]
    (inner,) = call(correct_kernel, "vvvvv", [(tile, f32, "v")], totals, name="correct")(
        got, local_grad, full, log_rate_t, residue_t
    )
    inner = exchange(inner, "ch")
    output, grad_key, grad_query, left, right, grad_residue, grad_rate, grad_gain = call(
        forward_kernel,
        "v" * 11,
        [
            (wide, bf16, "v"),
            (wide, bf16, "v"),
            (wide, bf16, "v"),
            (split, f32, "v"),
            (split, f32, "v"),
            (modes, f32, "v"),
            (modes, f32, "v"),
            ((1, COLS), f32, "v"),
        ],
        [pltpu.VMEM(split, f32), pltpu.VMEM(split, f32), *totals],
        name="forward",
    )(
        got,
        signal,
        inv,
        local_grad,
        stream,
        key_gate,
        query_gate,
        grad_output,
        gain,
        log_rate_t,
        residue_t,
    )
    (grad_stream,) = call(finish_kernel, "vvv", [(wide, bf16, "v")], name="finish")(
        inner, left, right
    )
    return (
        output,
        grad_stream,
        grad_key,
        grad_query,
        grad_gain[0],
        grad_residue.T,
        grad_rate.T,
    )


def solution(mesh):
    placed = (
        P("ctx", "ch"),
        P("ctx", "ch"),
        P("ctx", "ch"),
        P("ctx", "ch"),
        P("ch"),
        P("ch", None),
        P("ch", None),
    )
    return jax.shard_map(
        local,
        mesh=mesh,
        in_specs=placed,
        out_specs=(
            P("ctx", "ch"),
            P("ctx", "ch"),
            P("ctx", "ch"),
            P("ctx", "ch"),
            P("ch"),
            P("ch", None),
            P("ch", None),
        ),
        check_vma=False,
    )
```

```python
import math

import jax
import jax.numpy as jnp
from jax import lax
from jax.experimental import pallas as pl
from jax.experimental.pallas import tpu as pltpu
from jax.sharding import PartitionSpec as P

D = 4096
MODES = 16
ROWS = 512
COLS = 256
CHUNKS = 32
CH = 16
LANES = 128
SUB = 8
BLOCKS = ROWS // SUB
SPAN = 16
QUARTERS = ROWS // LANES
HALVES = COLS // LANES
GROUPS = MODES // SUB
epsilon = 1e-05
f32 = jnp.float32
bf16 = jnp.bfloat16


def call(kernel, ins, outs, scratch=(), limit=8, flops=1 << 22, name=None):
    held = {"v": pl.BlockSpec(memory_space=pltpu.VMEM), "a": pl.BlockSpec(memory_space=pltpu.HBM)}
    return pl.pallas_call(
        kernel,
        in_specs=[held[k] for k in ins],
        out_specs=tuple(held[k] for _, _, k in outs),
        out_shape=tuple(
            pltpu.HBM(s, d) if k == "a" else jax.ShapeDtypeStruct(s, d) for s, d, k in outs
        ),
        scratch_shapes=list(scratch),
        compiler_params=pltpu.CompilerParams(vmem_limit_bytes=limit << 20),
        cost_estimate=pl.CostEstimate(flops=flops, bytes_accessed=1 << 21, transcendentals=0),
        name=name,
    )


def lane(half):
    return pl.ds(half * LANES, LANES)


def lane_slice(half):
    return slice(half * LANES, (half + 1) * LANES)


def tiles(ref):
    return [[ref[g * SUB : (g + 1) * SUB, lane(h)] for h in range(HALVES)] for g in range(GROUPS)]


def each(fn, *args):
    return [[fn(*(a[g][h] for a in args)) for h in range(HALVES)] for g in range(GROUPS)]


def zeros_tiles():
    return [[jnp.zeros((SUB, LANES), f32) for _ in range(HALVES)] for _ in range(GROUPS)]


def fold_sublanes(parts):
    sub = lax.broadcasted_iota(jnp.int32, (SUB, LANES), 0)
    low4 = sub < 4
    low2 = (sub & 2) == 0
    low1 = (sub & 1) == 0
    four = []
    for k in range(4):
        a, b = parts[k], parts[k + 4]
        four.append(jnp.where(low4, a, b) + pltpu.roll(jnp.where(low4, b, a), 4, 0))
    two = []
    for k in range(2):
        a, b = four[k], four[k + 2]
        two.append(jnp.where(low2, a + pltpu.roll(a, 6, 0), b + pltpu.roll(b, 2, 0)))
    a, b = two
    return jnp.where(low1, a + pltpu.roll(a, 7, 0), b + pltpu.roll(b, 1, 0))


def row(ref, t, half):
    return ref[pl.ds(half * ROWS + t, SUB, stride=0), :]


def span(start, size, half):
    return (pl.ds(half * ROWS + start, size), slice(None))


def lane_totals(values):
    return jnp.broadcast_to(jnp.sum(values.T, axis=0, keepdims=True), (SUB, LANES))


def send_rows(ref, parts):
    sub = lax.broadcasted_iota(jnp.int32, (SUB, LANES), 0) & 3
    tile = parts[0]
    for k in range(1, QUARTERS):
        tile = jnp.where(sub == k, parts[k], tile)
    ref[...] = jnp.broadcast_to(tile[None, :QUARTERS], (CH, QUARTERS, LANES))


def columns(tile):
    turned = jnp.concatenate([tile, tile]).T
    return [turned[:, k : k + 1] for k in range(4)]


def square_kernel(stream_ref, send_ref):
    parts = []
    for k in range(QUARTERS):
        part = pl.ds(k * LANES, LANES)
        wide = [stream_ref[part, lane(h)].astype(f32) for h in range(HALVES)]
        parts.append(lane_totals(sum(v * v for v in wide)))
    send_rows(send_ref, parts)


def tile_rows(start, group, half):
    return pl.ds(start + (group * HALVES + half) * SUB, SUB)


def adjoint_kernel(
    query_ref,
    grad_ref,
    log_rate_ref,
    residue_ref,
    gain_ref,
    own_log_rate_ref,
    own_residue_ref,
    g_out,
    local_out,
    p_ref,
    w_ref,
    across_ref,
    across_lag_ref,
    gain_out,
    own_log_rate_out,
    own_residue_out,
    g_ref,
    local_ref,
    done,
):
    gain_out[...] = gain_ref[...]
    own_log_rate_out[...] = own_log_rate_ref[...]
    own_residue_out[...] = own_residue_ref[...]
    for h in range(HALVES):
        g_ref[span(0, ROWS, h)] = grad_ref[:, lane(h)].astype(f32) * query_ref[
            :, lane(h)
        ].astype(f32)
    g_copy = pltpu.make_async_copy(
        g_ref.reshape(HALVES * BLOCKS, SUB, LANES), g_out, done.at[1]
    )
    g_copy.start()
    rate = each(jnp.exp, tiles(log_rate_ref))
    lam = each(lambda v: jnp.exp(-v), rate)
    lam_block = each(lambda v: jnp.exp(v * (-float(SUB))), rate)
    res = tiles(residue_ref)

    def block(i, carry):
        p, w = carry
        index = BLOCKS - 1 - i
        base = pl.multiple_of(index * SUB, SUB)
        parts = [[None] * SUB for _ in range(HALVES)]
        near, near_w = None, None
        far, far_w = p, w
        for k in reversed(range(SUB)):
            rows = [row(g_ref, base + k, h) for h in range(HALVES)]
            p = [[lam[g][h] * p[g][h] + rows[h] for h in range(HALVES)] for g in range(GROUPS)]
            for h in range(HALVES):
                parts[h][k] = res[0][h] * p[0][h] + res[1][h] * p[1][h]
            if near is None:
                near = [rows, rows]
            else:
                a = each(lambda l, v: l * v, lam, near)
                if near_w is None:
                    near_w = a
                else:
                    near_w = each(lambda l, v, c: l * v + c, lam, near_w, a)
                near = [[a[g][h] + rows[h] for h in range(HALVES)] for g in range(GROUPS)]
        w = each(
            lambda n, l, v, q: n + l * (v + float(SUB) * q), near_w, lam_block, far_w, far
        )
        start = pl.multiple_of(index * (MODES * HALVES), SUB)
        for g in range(GROUPS):
            for h in range(HALVES):
                at = tile_rows(start, g, h)
                across_ref[at, :] = lam[g][h] * near[g][h]
                across_lag_ref[at, :] = lam[g][h] * (near_w[g][h] + near[g][h])
        for h in range(HALVES):
            local_ref[span(base, SUB, h)] = fold_sublanes(parts[h])
        return p, w

    p, w = lax.fori_loop(0, BLOCKS, block, (zeros_tiles(), zeros_tiles()))
    copy = pltpu.make_async_copy(local_ref, local_out, done.at[0])
    copy.start()
    for g in range(GROUPS):
        for h in range(HALVES):
            p_ref[g * SUB : (g + 1) * SUB, lane(h)] = p[g][h]
            w_ref[g * SUB : (g + 1) * SUB, lane(h)] = w[g][h]
    copy.wait()
    g_copy.wait()


def fill_fade(log_rate_ref, residue_ref, fade_ref, rate_ref, weight_ref):
    sub = lax.broadcasted_iota(jnp.int32, (SUB, LANES), 0)
    rate = each(jnp.exp, tiles(log_rate_ref))
    res = tiles(residue_ref)
    for g in range(GROUPS):
        for h in range(HALVES):
            rate_ref[tile_rows(0, g, h), :] = rate[g][h]
            weight_ref[tile_rows(0, g, h), :] = res[g][h]

    def block(at, carry):
        own_rate = rate_ref[pl.ds(at, SUB, stride=0), :]
        own_weight = weight_ref[pl.ds(at, SUB, stride=0), :]
        for k in range(SPAN // SUB):
            power = (sub + (k * SUB - SPAN)).astype(f32)
            rows = pl.ds(pl.multiple_of(at * SPAN + k * SUB, SUB), SUB)
            fade_ref[rows, :] = own_weight * jnp.exp(own_rate * power)
        return carry

    lax.fori_loop(0, MODES * HALVES, block, 0, unroll=8)


def state_kernel(
    recv_ref,
    stream_ref,
    key_ref,
    gain_ref,
    g_in,
    local_in,
    p_ref,
    w_ref,
    across_ref,
    across_lag_ref,
    log_rate_ref,
    send_ref,
    signal_out,
    inv_out,
    full_ref,
    signal_ref,
    inv_ref,
    local_ref,
    x_ref,
    u_ref,
    padded_ref,
    done,
):
    fetch = pltpu.make_async_copy(local_in, local_ref, done.at[0])
    fetch.start()
    wider_ref = padded_ref.reshape(HALVES * BLOCKS, 2 * SUB, LANES)
    fetch_g = pltpu.make_async_copy(g_in, wider_ref.at[:, pl.ds(0, SUB), :], done.at[3])
    fetch_g.start()
    total = jnp.sum(recv_ref[...], axis=0)
    inverse = columns(lax.rsqrt(total / D + epsilon))
    gain = gain_ref[...]
    for k in range(4):
        part = pl.ds(k * LANES, LANES)
        inv = jnp.broadcast_to(inverse[k], (LANES, LANES))
        inv_ref[part, :] = inv
        for h in range(HALVES):
            unit = stream_ref[part, lane(h)].astype(f32) * inv
            key = key_ref[part, lane(h)].astype(f32)
            own = span(k * LANES, LANES, h)
            u_ref[own] = key * unit
            signal = key * (unit * gain[:, lane_slice(h)])
            full_ref[own] = signal
            narrow = signal.astype(bf16)
            signal_ref[own] = narrow
            x_ref[own] = narrow.astype(f32)
    stores = [
        pltpu.make_async_copy(signal_ref, signal_out, done.at[1]),
        pltpu.make_async_copy(inv_ref, inv_out, done.at[2]),
    ]
    for copy in stores:
        copy.start()
    lam = each(lambda v: jnp.exp(-jnp.exp(v)), tiles(log_rate_ref))

    def block(i, carry):
        state, moment, plain, first, second = carry
        base = pl.multiple_of(i * SUB, SUB)
        start = pl.multiple_of(i * (MODES * HALVES), SUB)
        near = [[across_ref[tile_rows(start, g, h), :] for h in range(HALVES)] for g in range(GROUPS)]
        near_lag = [
            [across_lag_ref[tile_rows(start, g, h), :] for h in range(HALVES)]
            for g in range(GROUPS)
        ]
        first = each(lambda f, s, n: f + s * n, first, state, near)
        second = each(
            lambda f, s, n, m, v: f + (s * n + m * v), second, state, near_lag, moment, near
        )
        for h in range(HALVES):
            wider = pl.multiple_of((h * BLOCKS + i) * 2 * SUB, 2 * SUB)
            padded_ref[pl.ds(wider + SUB, SUB), :] = jnp.zeros((SUB, LANES), f32)
        for k in range(SUB):
            xs = [row(x_ref, base + k, h) for h in range(HALVES)]
            us = [row(u_ref, base + k, h) for h in range(HALVES)]
            a = each(lambda l, v: l * v, lam, state)
            moment = each(lambda l, v, c: l * v + c, lam, moment, a)
            state = [[a[g][h] + xs[h] for h in range(HALVES)] for g in range(GROUPS)]
            plain = [
                [lam[g][h] * plain[g][h] + us[h] for h in range(HALVES)] for g in range(GROUPS)
            ]
        return state, moment, plain, first, second

    zero = zeros_tiles
    start = (zero(), zero(), zero(), zero(), zero())
    state, moment, plain, first, second = lax.fori_loop(0, BLOCKS, block, start, unroll=4)


    def inside(i, carry):
        sums, gains = carry
        base = pl.multiple_of(i * SUB, SUB)
        new_sums, new_gains = [], []
        for h in range(HALVES):
            at = span(base, SUB, h)
            x = x_ref[at]
            new_gains.append(gains[h] + u_ref[at] * local_ref[at])
            wider = pl.multiple_of((h * BLOCKS + i) * 2 * SUB, 2 * SUB)
            own = [
                sums[h][d] + x * padded_ref[pl.ds(wider + d, SUB), :] for d in range(SUB)
            ]
            new_sums.append(own)
        return new_sums, new_gains

    fetch.wait()
    fetch_g.wait()
    none = jnp.zeros((SUB, LANES), f32)
    sums, gains = lax.fori_loop(
        0, BLOCKS, inside, ([[none] * SUB for _ in range(HALVES)], [none] * HALVES), unroll=8
    )
    near, near_lag = zero(), zero()
    for d in reversed(range(SUB)):
        each_sum = [
            jnp.broadcast_to(jnp.sum(sums[h][d], axis=0, keepdims=True), (SUB, LANES))
            for h in range(HALVES)
        ]
        a = each(lambda l, v: l * v, lam, near)
        near_lag = each(lambda l, v, c: l * v + c, lam, near_lag, a)
        near = [[a[g][h] + each_sum[h] for h in range(HALVES)] for g in range(GROUPS)]
    first = each(lambda f, n: f + n, first, near)
    second = each(lambda f, n: f + n, second, near_lag)
    last = [gains, [jnp.zeros((SUB, LANES), f32)] * HALVES]
    sent = [state, plain, moment, tiles(p_ref), tiles(w_ref), first, second, last]
    flat_ref = send_ref.reshape(CHUNKS * SUB, LANES)
    for q in range(SUB):
        for g in range(GROUPS):
            for h in range(HALVES):
                at = g * SUB * HALVES * SUB + h * SUB + q
                flat_ref[pl.ds(at, SUB, stride=HALVES * SUB), :] = sent[q][g][h]
    for store in stores:
        store.wait()


def shifted(value, k):
    index = lax.broadcasted_iota(jnp.int32, (CHUNKS, LANES), 0)
    return jnp.where(index >= k, pltpu.roll(value, k, 0), 0.0)


def shifted_back(value, k):
    index = lax.broadcasted_iota(jnp.int32, (CHUNKS, LANES), 0)
    return jnp.where(index < CHUNKS - k, pltpu.roll(value, CHUNKS - k, 0), 0.0)


def owner_kernel(recv_ref, log_rate_ref, residue_ref, send_ref):
    flat_ref = recv_ref.reshape(CHUNKS * SUB, LANES)
    state, plain, moment, p, w, first, second, gains = (
        flat_ref[pl.ds(q, CHUNKS, stride=SUB), :] for q in range(SUB)
    )
    rate = jnp.exp(log_rate_ref[...])
    res = residue_ref[...]
    lam = jnp.exp(-rate)
    whole, whole_u, whole_q, back = state, plain, moment, p
    for step in (1, 2, 4, 8, 16):
        far = jnp.exp(rate * (-float(ROWS * step)))
        before = shifted(whole, step)
        whole_q = whole_q + far * (shifted(whole_q, step) + float(ROWS * step) * before)
        whole = whole + far * before
        whole_u = whole_u + far * shifted(whole_u, step)
        back = back + far * shifted_back(back, step)
    into, into_u, into_q = shifted(whole, 1), shifted(whole_u, 1), shifted(whole_q, 1)
    into_p = shifted_back(back, 1)
    scale = 1.0 / math.sqrt(ROWS * CHUNKS)
    grad_residue = jnp.sum(first + lam * (into * p), axis=0, keepdims=True)
    weighted = jnp.sum(second + lam * ((w + p) * into + p * into_q), axis=0, keepdims=True)
    grad_gain = jnp.sum(gains + res * (lam * (into_u * p)), axis=0, keepdims=True)
    shape = (CHUNKS, LANES)
    rows = [
        into,
        into_p,
        jnp.broadcast_to(grad_residue * scale, shape),
        jnp.broadcast_to(-rate * res * weighted * scale, shape),
        jnp.broadcast_to(grad_gain * scale, shape),
    ]
    rows += [jnp.zeros(shape, f32)] * (SUB - len(rows))
    flat_ref = send_ref.reshape(CHUNKS * SUB, LANES)
    for q in range(SUB):
        flat_ref[pl.ds(q, CHUNKS, stride=SUB), :] = rows[q]


def received(ref, q):
    stride = HALVES * SUB
    flat_ref = ref.reshape(CHUNKS * SUB, LANES)
    return [
        [
            flat_ref[pl.ds(g * SUB * stride + h * SUB + q, SUB, stride=stride), :]
            for h in range(HALVES)
        ]
        for g in range(GROUPS)
    ]


def fill_totals(
    recv_ref,
    local_ref,
    log_rate_ref,
    residue_ref,
    total_ref,
    into_ref,
    fade_ref,
    rate_ref,
    weight_ref,
):
    fill_fade(log_rate_ref, residue_ref, fade_ref, rate_ref, weight_ref)
    into = received(recv_ref, 1)
    step = each(lambda v: jnp.exp(jnp.exp(v) * (-float(SPAN))), tiles(log_rate_ref))
    spans = ROWS // SPAN
    for b in reversed(range(spans)):
        for g in range(GROUPS):
            for h in range(HALVES):
                into_ref[tile_rows(b * MODES * HALVES, g, h), :] = into[g][h]
        into = each(lambda l, v: l * v, step, into)
    places = [
        [(g * HALVES + h) * SUB + m for g in range(GROUPS) for m in range(SUB)]
        for h in range(HALVES)
    ]

    def block(b, carry):
        for h in range(HALVES):
            rows = [into_ref[pl.ds(b * MODES * HALVES + at, SUB, stride=0), :] for at in places[h]]
            for k in range(SPAN // SUB):
                own = span(pl.multiple_of(b * SPAN + k * SUB, SUB), SUB, h)
                terms = [
                    fade_ref[pl.ds(at * SPAN + k * SUB, SUB), :] * rows[m]
                    for m, at in enumerate(places[h])
                ]
                while len(terms) > 1:
                    terms = [a + b for a, b in zip(terms[::2], terms[1::2])]
                total_ref[own] = local_ref[own] + terms[0]
        return carry

    lax.fori_loop(0, spans, block, 0, unroll=4)


def correct_kernel(
    recv_ref,
    local_ref,
    full_ref,
    log_rate_ref,
    residue_ref,
    send_ref,
    total_ref,
    into_ref,
    fade_ref,
    rate_ref,
    weight_ref,
):
    fill_totals(
        recv_ref,
        local_ref,
        log_rate_ref,
        residue_ref,
        total_ref,
        into_ref,
        fade_ref,
        rate_ref,
        weight_ref,
    )
    parts = []
    for k in range(QUARTERS):
        own = [span(k * LANES, LANES, h) for h in range(HALVES)]
        parts.append(lane_totals(sum(total_ref[at] * full_ref[at] for at in own)))
    send_rows(send_ref, parts)


def forward_kernel(
    recv_ref,
    signal_ref,
    inv_ref,
    local_ref,
    stream_ref,
    key_ref,
    query_ref,
    grad_ref,
    gain_ref,
    log_rate_ref,
    residue_ref,
    output_ref,
    grad_key_ref,
    grad_query_ref,
    left_ref,
    right_ref,
    grad_residue_ref,
    grad_rate_ref,
    grad_gain_ref,
    conv_ref,
    x_ref,
    total_ref,
    into_ref,
    fade_ref,
    rate_ref,
    weight_ref,
):
    fill_totals(
        recv_ref,
        local_ref,
        log_rate_ref,
        residue_ref,
        total_ref,
        into_ref,
        fade_ref,
        rate_ref,
        weight_ref,
    )
    x_ref[...] = signal_ref[...].astype(f32)
    lam = each(lambda v: jnp.exp(-jnp.exp(v)), tiles(log_rate_ref))
    res = tiles(residue_ref)

    def block(i, state):
        base = pl.multiple_of(i * SUB, SUB)
        parts = [[None] * SUB for _ in range(HALVES)]
        for k in range(SUB):
            xs = [row(x_ref, base + k, h) for h in range(HALVES)]
            state = [
                [lam[g][h] * state[g][h] + xs[h] for h in range(HALVES)] for g in range(GROUPS)
            ]
            for h in range(HALVES):
                parts[h][k] = res[0][h] * state[0][h] + res[1][h] * state[1][h]
        for h in range(HALVES):
            conv_ref[span(base, SUB, h)] = fold_sublanes(parts[h])
        return state

    lax.fori_loop(0, BLOCKS, block, received(recv_ref, 0))
    gain = gain_ref[...]
    for k in range(4):
        part = pl.ds(k * LANES, LANES)
        inv = inv_ref[part, :]
        for h in range(HALVES):
            at = (part, lane(h))
            own = span(k * LANES, LANES, h)
            conv = conv_ref[own]
            output_ref[at] = (query_ref[at].astype(f32) * conv).astype(bf16)
            grad_query_ref[at] = (grad_ref[at].astype(f32) * conv).astype(bf16)
            unit = stream_ref[at].astype(f32) * inv
            total = total_ref[own]
            own_gain = gain[:, lane_slice(h)]
            grad_key_ref[at] = (total * (unit * own_gain)).astype(bf16)
            left_ref[own] = inv * (total * key_ref[at].astype(f32) * own_gain)
            right_ref[own] = inv * unit
    for q, ref in ((2, grad_residue_ref), (3, grad_rate_ref)):
        found = received(recv_ref, q)
        for g in range(GROUPS):
            for h in range(HALVES):
                ref[g * SUB : (g + 1) * SUB, lane(h)] = found[g][h]
    found = received(recv_ref, 4)
    for h in range(HALVES):
        grad_gain_ref[:, lane(h)] = jnp.sum(found[0][h] + found[1][h], axis=0, keepdims=True)


def finish_kernel(recv_ref, left_ref, right_ref, grad_stream_ref):
    inner = columns(jnp.sum(recv_ref[...], axis=0) / D)
    for k in range(QUARTERS):
        part = pl.ds(k * LANES, LANES)
        across = jnp.broadcast_to(inner[k], (LANES, LANES))
        for h in range(HALVES):
            own = span(k * LANES, LANES, h)
            value = left_ref[own] - right_ref[own] * across
            grad_stream_ref[part, lane(h)] = value.astype(bf16)


def in_hbm(value):
    return pltpu.with_memory_space_constraint(value, pltpu.HBM)


def exchange(value, axis):
    return lax.all_to_all(value, axis, split_axis=0, concat_axis=0, tiled=True)


def local(stream, key_gate, query_gate, grad_output, norm_gain, residue, log_rate):
    wide = (ROWS, COLS)
    split = (HALVES * ROWS, LANES)
    modes = (MODES, COLS)
    tile = (CH, QUARTERS, LANES)
    (squares,) = call(square_kernel, "v", [(tile, f32, "v")], name="square")(stream)
    squares = exchange(squares, "ch")
    log_rate_t = log_rate.T
    residue_t = residue.T
    me = lax.axis_index("ctx")
    log_rate_own = lax.dynamic_slice_in_dim(log_rate_t.reshape(CHUNKS, LANES), me, 1, 0)
    residue_own = lax.dynamic_slice_in_dim(residue_t.reshape(CHUNKS, LANES), me, 1, 0)
    table = (BLOCKS * MODES * HALVES, LANES)
    packed = (CHUNKS, SUB, LANES)
    own = (1, LANES)
    (
        grad_conv,
        local_grad,
        p,
        w,
        across,
        across_lag,
        gain,
        log_rate_own,
        residue_own,
    ) = call(
        adjoint_kernel,
        "v" * 7,
        [
            ((HALVES * BLOCKS, SUB, LANES), f32, "a"),
            (split, f32, "a"),
            (modes, f32, "v"),
            (modes, f32, "v"),
            (table, f32, "v"),
            (table, f32, "v"),
            ((1, COLS), f32, "v"),
            (own, f32, "v"),
            (own, f32, "v"),
        ],
        [pltpu.VMEM(split, f32), pltpu.VMEM(split, f32), pltpu.SemaphoreType.DMA((2,))],
        name="adjoint",
    )(
        query_gate,
        grad_output,
        log_rate_t,
        residue_t,
        norm_gain[None, :],
        log_rate_own,
        residue_own,
    )
    rows = (ROWS, LANES)
    sent, signal, inv, full = call(
        state_kernel,
        "vvvvaavvvvv",
        [(packed, f32, "v"), (split, bf16, "a"), (rows, f32, "a"), (split, f32, "v")],
        [
            pltpu.VMEM(split, bf16),
            pltpu.VMEM(rows, f32),
            pltpu.VMEM(split, f32),
            pltpu.VMEM(split, f32),
            pltpu.VMEM(split, f32),
            pltpu.VMEM((2 * HALVES * ROWS, LANES), f32),
            pltpu.SemaphoreType.DMA((4,)),
        ],
        name="state",
    )(
        squares,
        stream,
        key_gate,
        gain,
        in_hbm(grad_conv),
        in_hbm(local_grad),
        p,
        w,
        across,
        across_lag,
        log_rate_t,
    )
    got = exchange(sent, "ctx")
    (sent,) = call(owner_kernel, "vvv", [(packed, f32, "v")], name="owner")(
        got, log_rate_own, residue_own
    )
    got = exchange(sent, "ctx")
    totals = [
        pltpu.VMEM(split, f32),
        pltpu.VMEM((ROWS // SPAN * MODES * HALVES, LANES), f32),
        pltpu.VMEM((MODES * HALVES * SPAN, LANES), f32),
        pltpu.VMEM((MODES * HALVES, LANES), f32),
        pltpu.VMEM((MODES * HALVES, LANES), f32),
    ]
    (inner,) = call(correct_kernel, "vvvvv", [(tile, f32, "v")], totals, name="correct")(
        got, local_grad, full, log_rate_t, residue_t
    )
    inner = exchange(inner, "ch")
    output, grad_key, grad_query, left, right, grad_residue, grad_rate, grad_gain = call(
        forward_kernel,
        "v" * 11,
        [
            (wide, bf16, "v"),
            (wide, bf16, "v"),
            (wide, bf16, "v"),
            (split, f32, "v"),
            (split, f32, "v"),
            (modes, f32, "v"),
            (modes, f32, "v"),
            ((1, COLS), f32, "v"),
        ],
        [pltpu.VMEM(split, f32), pltpu.VMEM(split, f32), *totals],
        name="forward",
    )(
        got,
        signal,
        inv,
        local_grad,
        stream,
        key_gate,
        query_gate,
        grad_output,
        gain,
        log_rate_t,
        residue_t,
    )
    (grad_stream,) = call(finish_kernel, "vvv", [(wide, bf16, "v")], name="finish")(
        inner, left, right
    )
    return (
        output,
        grad_stream,
        grad_key,
        grad_query,
        grad_gain[0],
        grad_residue.T,
        grad_rate.T,
    )


def solution(mesh):
    placed = (
        P("ctx", "ch"),
        P("ctx", "ch"),
        P("ctx", "ch"),
        P("ctx", "ch"),
        P("ch"),
        P("ch", None),
        P("ch", None),
    )
    return jax.shard_map(
        local,
        mesh=mesh,
        in_specs=placed,
        out_specs=(
            P("ctx", "ch"),
            P("ctx", "ch"),
            P("ctx", "ch"),
            P("ctx", "ch"),
            P("ch"),
            P("ch", None),
            P("ch", None),
        ),
        check_vma=False,
    )
```
